256 devices in a mesh: tm: 64 (over z, x, core), chan: 4 (over y).
Axes of the slice: x: 4, y: 4, z: 8, core: 2. Of those that a mesh axis runs over, the one named last changes fastest.
Arguments:
- data: bfloat16 [384, 131072], P('chan', 'tm'), may hold values from 0.049804688 to 2
- motifs: bfloat16 [384, 2048], P('chan', 'tm'), may hold values from 9.727478e-05 to 0.001953125
- loadings: float32 [64, 131072], P(None, 'tm'), as said below
Outputs:
- factors_now: float32 [64, 131072], P(None, 'tm')
The draws below stay inside these ranges and needn't reach their ends.
Inputs may be any that keep to these rules, and one draw needn't show every extreme that they name: `loadings`: every entry is positive.
All inputs are finite; a program needn't handle non-finite values.
Results may differ from the reference program's by a relative error of at most 0.0003.
Values may be sent and summed in bfloat16 or wider, within the bound.
A program may use at most 128 MiB of HBM per device.

```python
import math
import jax
import jax.numpy as jnp
from jax import lax

CHANNELS = 384
FACTORS = 64
LAGS = 32
ITERS = 3
TOTAL = 131072


def draw_loadings(key, part):
    first_key, second_key = jax.random.split(jax.random.fold_in(key, 7))
    ramp = 1.0 + 2.0 * jnp.arange(TOTAL, dtype=jnp.float32) / (TOTAL - 1)
    base = jax.random.uniform(first_key, (FACTORS, TOTAL), jnp.float32, 0.2, 1.0)
    scales = jnp.exp(jax.random.uniform(second_key, (FACTORS, 1), jnp.float32) * jnp.log(4.0))
    return (base * scales * ramp[None, :]).astype(jnp.float32)


def levels(stream_key, extent, cuts, least, top_value):
    def one(position, shards_of):
        heights = jax.random.uniform(jax.random.fold_in(jax.random.fold_in(stream_key, 6), position), (shards_of,), jnp.float32, least / len(cuts), top_value / len(cuts))
        return jnp.repeat(jnp.exp(heights), extent[position] // shards_of).reshape((-1,) + (1,) * (len(extent) - position - 1))

    level = one(*cuts[0])
    for cut in cuts[1:]:
        level = level * one(*cut)
    return level


def setup_inputs(seed: int = 0) -> dict:
    key_of = jax.random.split(jax.random.key(seed), 4)
    return {
        "data": jnp.clip(jnp.exp(math.log(2.0) - 3.6927934 * jax.random.uniform(key_of[0], (CHANNELS, TOTAL), jnp.float32) ** levels(key_of[0], (CHANNELS, TOTAL), ((0, 4), (1, 64)), -0.2, 0.2)), 0.049804688, 2.0).astype(jnp.bfloat16),
        "motifs": jnp.clip(jnp.exp(math.log(0.001953125) - 2.9996462 * jax.random.uniform(key_of[1], (CHANNELS, FACTORS * LAGS), jnp.float32) ** levels(key_of[1], (CHANNELS, FACTORS * LAGS), ((0, 4), (1, 64)), -0.2, 0.2)), 9.72747802734375e-05, 0.001953125).astype(jnp.bfloat16),
        "loadings": draw_loadings(jax.random.fold_in(key_of[3], 71), 0),
    }


penalty_weight = 0.2


def shift_back(field, offset):
    if offset == 0:
        return field
    return jnp.concatenate([field[:, offset:], jnp.zeros((field.shape[0], offset), field.dtype)], 1)


def shift_fore(field, offset):
    if offset == 0:
        return field
    cols = field.shape[1]
    return jnp.concatenate([jnp.zeros((field.shape[0], offset), field.dtype), field[:, :cols - offset]], 1)


def reference(data, motifs, loadings):
    signal = data.astype(jnp.float32)
    motif_all = motifs.astype(jnp.float32).reshape(CHANNELS, FACTORS, LAGS)
    length_all = signal.shape[1]
    hp = lax.Precision.HIGHEST

    def correlate(field):
        result = jnp.zeros((FACTORS, length_all), jnp.float32)
        for offset in range(LAGS):
            result = result + jnp.dot(motif_all[:, :, offset].T, shift_back(field, offset), precision=hp, preferred_element_type=jnp.float32)
        return result

    numerator = correlate(signal)
    factors_now = loadings
    off_mask = 1.0 - jnp.eye(FACTORS, dtype=jnp.float32)
    for sweep in range(ITERS):
        gram_mat = jnp.dot(factors_now, factors_now.T, precision=hp, preferred_element_type=jnp.float32) / length_all
        rounded = lax.optimization_barrier(factors_now.astype(jnp.bfloat16)).astype(jnp.float32)
        recon = jnp.zeros((CHANNELS, length_all), jnp.float32)
        for offset in range(LAGS):
            recon = recon + jnp.dot(motif_all[:, :, offset], shift_fore(rounded, offset), precision=hp, preferred_element_type=jnp.float32)
        recon = lax.optimization_barrier(recon.astype(jnp.bfloat16)).astype(jnp.float32)
        denominator = correlate(recon)
        penalty = penalty_weight * jnp.dot(gram_mat * off_mask, factors_now, precision=hp, preferred_element_type=jnp.float32)
        factors_now = factors_now * numerator / (denominator + penalty)
    return factors_now
```

```python
import functools

import jax
import jax.numpy as jnp
from jax import lax
from jax.experimental import pallas as pl
from jax.experimental.pallas import tpu as pltpu
from jax.sharding import PartitionSpec as P

FACTORS = 64
LAGS = 32
ITERS = 3
LANES = 128
HALO = LAGS
penalty_weight = 0.2

F32 = jnp.float32
BF16 = jnp.bfloat16
MESH = pl.DeviceIdType.MESH
NT = (((1,), (1,)), ((), ()))
TN = (((0,), (0,)), ((), ()))

NX = 4
NC = 2


def kernel(nz, ny, total, w_ref, x_ref, h_ref, out_ref, df, hst, r, r4, q, num, fa,
           halo_src, halo_l, halo_r, gsrc, cbuf, part, xbuf, ybuf, zbuf, gtot, fin,
           send_sem, recv_sem):
    own = h_ref.shape[1]
    tm = lax.axis_index("tm")
    y = lax.axis_index("chan")
    core = tm % NC
    x = (tm // NC) % NX
    z = tm // (NC * NX)
    ntm = nz * NX * NC

    def at(zz, xx, cc, yy):
        return ((zz * NX + xx) * NC + cc, yy)

    spot = tm * ny + y
    right_spot = (spot + 1) % (ntm * ny)
    left_spot = (spot + ntm * ny - 1) % (ntm * ny)
    right = (right_spot // ny, right_spot % ny)
    left = (left_spot // ny, left_spot % ny)
    first = spot == 0
    last = spot == ntm * ny - 1

    other = at(z, x, 1 - core, y)
    along_x = [at(z, (x + d) % NX, core, y) for d in range(1, NX)]
    along_y = [at(z, x, core, (y + d) % ny) for d in range(1, ny)]
    along_z = [at((z + d) % nz, x, core, y) for d in range(1, nz)]

    barrier = pltpu.get_barrier_semaphore()
    everyone = [other, left, right] + along_x + along_y + along_z
    for device in everyone:
        pl.semaphore_signal(barrier, inc=1, device_id=device, device_id_type=MESH)
    pl.semaphore_wait(barrier, len(everyone))

    count = [0]

    def remote(src, dst, device):
        slot = count[0]
        count[0] += 1
        copy = pltpu.make_async_remote_copy(
            src_ref=src, dst_ref=dst, send_sem=send_sem.at[slot], recv_sem=recv_sem.at[slot],
            device_id=device, device_id_type=MESH)
        copy.start()
        return copy

    def correlate():
        rows = own + 16
        for a in range(4):
            r4[:, 512 * a:512 * a + 512] = r[8 * a:8 * a + rows, :]
        acc = None
        for a in range(4):
            d = lax.dot_general(r4[:, 512 * a:512 * a + 512], w_ref[512 * a:512 * a + 512, :], NT,
                                preferred_element_type=F32)
            acc = d if acc is None else acc + d
        q[...] = acc
        s = q[0:own + 8, 0:LANES]
        for b in range(1, 4):
            s = s + q[2 * b:2 * b + own + 8, LANES * b:LANES * b + LANES]
        return s[0:own, 0:FACTORS] + s[1:own + 1, FACTORS:2 * FACTORS]

    def convolve():
        rows = own + HALO
        for j in range(LAGS // 2):
            hst[:, LANES * j:LANES * j + LANES] = df[HALO - 2 * j:HALO - 2 * j + rows, :].astype(BF16)
        r[0:rows, :] = jnp.dot(hst[...], w_ref[...], preferred_element_type=F32).astype(BF16)
        tail = r[own:rows, :]
        r[own:rows, :] = jnp.where(last, jnp.zeros_like(tail), tail)

    def put_field(field):
        df[HALO:HALO + own, 0:FACTORS] = field
        df[HALO + 1:HALO + own + 1, FACTORS:2 * FACTORS] = field
        hi = field.astype(BF16)
        lo = (field - hi.astype(F32)).astype(BF16)
        fa[:, 0:FACTORS] = hi
        fa[:, FACTORS:2 * FACTORS] = lo

    def put_halos(it):
        from_left = halo_l[it]
        from_left = jnp.where(first, jnp.zeros_like(from_left), from_left)
        from_right = halo_r[it]
        df[0:HALO, 0:FACTORS] = from_left
        df[1:HALO + 1, FACTORS:2 * FACTORS] = from_left
        df[HALO + own:own + 2 * HALO, 0:FACTORS] = from_right
        df[HALO + own + 1:own + 2 * HALO, FACTORS:2 * FACTORS] = from_right[0:HALO - 1]

    def send_halos(it, field):
        halo_src[it, 0] = field[0:HALO]
        halo_src[it, 1] = field[own - HALO:own]
        return [remote(halo_src.at[it, 0], halo_r.at[it], left),
                remote(halo_src.at[it, 1], halo_l.at[it], right)]

    row_id = lax.broadcasted_iota(jnp.int32, (FACTORS, FACTORS), 0)
    col_id = lax.broadcasted_iota(jnp.int32, (FACTORS, FACTORS), 1)
    off_mask = jnp.where(row_id == col_id, 0.0, penalty_weight / total).astype(F32)

    df[0:8, :] = jnp.zeros((8, 2 * FACTORS), F32)
    r[...] = x_ref[...]
    field = h_ref[...].T
    for it in range(ITERS):
        pending = send_halos(it, field)
        put_field(field)
        gg = lax.dot_general(fa[...], fa[...], TN, preferred_element_type=F32)
        gram = (gg[0:FACTORS, 0:FACTORS] + gg[0:FACTORS, FACTORS:] + gg[FACTORS:, 0:FACTORS]
                + gg[FACTORS:, FACTORS:])
        packed = jnp.concatenate([gram[0:32], gram[32:64]], axis=1)
        gsrc[it, 0] = packed[0:16]
        gsrc[it, 1] = packed[16:32]
        c0 = remote(gsrc.at[it, 1 - core], cbuf.at[it], other)
        c0.wait_recv()
        part[it, 0] = gsrc[it, core] + cbuf[it]
        cx = [remote(part.at[it, 0], xbuf.at[it, d], dev) for d, dev in enumerate(along_x)]
        if it == 0:
            num[...] = correlate()
        for c in cx:
            c.wait_recv()
        part[it, 1] = part[it, 0] + xbuf[it, 0] + xbuf[it, 1] + xbuf[it, 2]
        cy = [remote(part.at[it, 1], ybuf.at[it, d], dev) for d, dev in enumerate(along_y)]
        for c in pending:
            c.wait_recv()
        put_halos(it)
        convolve()
        for c in cy:
            c.wait_recv()
        acc = part[it, 1]
        for d in range(ny - 1):
            acc = acc + ybuf[it, d]
        part[it, 2] = acc
        cz = [remote(part.at[it, 2], zbuf.at[it, d], dev) for d, dev in enumerate(along_z)]
        denom = correlate()
        for c in cz:
            c.wait_recv()
        acc = part[it, 2]
        for d in range(nz - 1):
            acc = acc + zbuf[it, d]
        part[it, 3] = acc
        c1 = remote(part.at[it, 3], gtot.at[it], other)
        c1.wait_recv()
        mine, theirs = part[it, 3], gtot[it]
        low = jnp.where(core == 0, mine, theirs)
        high = jnp.where(core == 0, theirs, mine)
        packed = jnp.concatenate([low, high], axis=0)
        off = jnp.concatenate([packed[:, 0:FACTORS], packed[:, FACTORS:]], axis=0) * off_mask
        off_hi = off.astype(BF16)
        off_lo = (off - off_hi.astype(F32)).astype(BF16)
        penalty = (jnp.dot(fa[...], jnp.concatenate([off_hi, off_hi], axis=0), preferred_element_type=F32)
                   + jnp.dot(fa[:, 0:FACTORS], off_lo, preferred_element_type=F32))
        field = df[HALO:HALO + own, 0:FACTORS] * num[...] / (denom + penalty)
        for c in [c0, c1] + pending + cx + cy + cz:
            c.wait_send()

    fin[...] = field.T
    columns = pl.ds(pl.multiple_of(y * own, own), own)
    out_ref[:, columns] = fin[...]
    copies = [remote(fin, out_ref.at[:, columns], dev) for dev in along_y]
    for c in copies:
        c.wait()


def on_device(data, motifs, loadings):
    ntm, ny = lax.axis_size("tm"), lax.axis_size("chan")
    blocks, steps = data.shape
    own = steps // ny
    y = lax.axis_index("chan")
    pad = LANES - blocks
    piece = jnp.pad(motifs.T, ((0, 0), (0, pad)))
    everything = lax.all_gather(piece, ("chan", "tm")).reshape(ny, ntm, LAGS, LANES)
    w = jnp.transpose(everything, (2, 1, 0, 3)).reshape(LAGS * FACTORS, ny * LANES)
    pairs = [(i, i - 1) for i in range(1, ntm)]
    rim = lax.ppermute(data[:, :HALO], "tm", pairs)
    wide = jnp.concatenate([data, rim], 1)
    tiles = jnp.stack([wide[:, i * own:i * own + own + HALO] for i in range(ny)])
    tiles = lax.all_to_all(tiles, "chan", 0, 0, tiled=True)
    x = jnp.transpose(jnp.pad(tiles, ((0, 0), (0, pad), (0, 0))), (2, 0, 1)).reshape(own + HALO, ny * LANES)
    x = jnp.pad(x, ((0, 16), (0, 0)))
    mine = lax.dynamic_slice_in_dim(loadings, y * own, own, 1)

    nz = ntm // (NX * NC)
    V = pl.BlockSpec(memory_space=pltpu.VMEM)
    copies = ITERS * (4 + (NX - 1) + (ny - 1) + (nz - 1)) + (ny - 1)
    vm = pltpu.VMEM
    return pl.pallas_call(
        functools.partial(kernel, nz, ny, float(steps * ntm)),
        out_shape=jax.ShapeDtypeStruct((FACTORS, steps), F32),
        in_specs=[V, V, V],
        out_specs=V,
        scratch_shapes=[
            vm((own + 2 * HALO, 2 * FACTORS), F32),
            vm((own + HALO, LAGS * FACTORS), BF16),
            vm((own + HALO + 16, ny * LANES), BF16),
            vm((own + 16, 4 * ny * LANES), BF16),
            vm((own + 16, 4 * LANES), F32),
            vm((own, FACTORS), F32),
            vm((own, 2 * FACTORS), BF16),
            vm((ITERS, 2, HALO, FACTORS), F32),
            vm((ITERS, HALO, FACTORS), F32),
            vm((ITERS, HALO, FACTORS), F32),
            vm((ITERS, 2, 16, LANES), F32),
            vm((ITERS, 16, LANES), F32),
            vm((ITERS, 4, 16, LANES), F32),
            vm((ITERS, NX - 1, 16, LANES), F32),
            vm((ITERS, ny - 1, 16, LANES), F32),
            vm((ITERS, nz - 1, 16, LANES), F32),
            vm((ITERS, 16, LANES), F32),
            vm((FACTORS, own), F32),
            pltpu.SemaphoreType.DMA((copies,)),
            pltpu.SemaphoreType.DMA((copies,)),
        ],
        compiler_params=pltpu.CompilerParams(collective_id=0, has_side_effects=True),
    )(w, x, mine)


def solution(mesh):
    in_specs = (P("chan", "tm"), P("chan", "tm"), P(None, "tm"))
    out_specs = P(None, "tm")
    return jax.shard_map(
        on_device, mesh=mesh, in_specs=in_specs, out_specs=out_specs, check_vma=False
    )
```

```python
import functools

import jax
import jax.numpy as jnp
from jax import lax
from jax.experimental import pallas as pl
from jax.experimental.pallas import tpu as pltpu
from jax.sharding import PartitionSpec as P

FACTORS = 64
LAGS = 32
ITERS = 3
LANES = 128
HALO = LAGS
penalty_weight = 0.2

F32 = jnp.float32
BF16 = jnp.bfloat16
MESH = pl.DeviceIdType.MESH
NT = (((1,), (1,)), ((), ()))
TN = (((0,), (0,)), ((), ()))

NX = 4
NC = 2


def kernel(nz, ny, total, m_ref, x_ref, h_ref, out_ref, src, got, wf, w_ref, tiles, rim_src, rim,
           df, hst, r, r4, q, num, fa, halo_src, halo_l, halo_r, gsrc, cbuf, part, xybuf, zbuf, gtot,
           fin, send_sem, recv_sem):
    blocks = m_ref.shape[0]
    own = h_ref.shape[1] // ny
    tm = lax.axis_index("tm")
    y = lax.axis_index("chan")
    core = tm % NC
    x = (tm // NC) % NX
    z = tm // (NC * NX)
    ntm = nz * NX * NC

    def at(zz, xx, cc, yy):
        return ((zz * NX + xx) * NC + cc, yy)

    spot = tm * ny + y
    right_spot = (spot + 1) % (ntm * ny)
    left_spot = (spot + ntm * ny - 1) % (ntm * ny)
    right = (right_spot // ny, right_spot % ny)
    left = (left_spot // ny, left_spot % ny)
    first = spot == 0
    last = spot == ntm * ny - 1

    other = at(z, x, 1 - core, y)
    along_x = [at(z, (x + d) % NX, core, y) for d in range(1, NX)]
    along_y = [at(z, x, core, (y + d) % ny) for d in range(1, ny)]
    across = [at(z, (x + d) % NX, core, (y + e) % ny) for d in range(NX) for e in range(ny) if d or e]
    along_z = [at((z + d) % nz, x, core, y) for d in range(1, nz)]

    barrier = pltpu.get_barrier_semaphore()
    everyone = [other, left, right] + across + along_z
    for device in everyone:
        pl.semaphore_signal(barrier, inc=1, device_id=device, device_id_type=MESH)
    pl.semaphore_wait(barrier, len(everyone))

    count = [0]

    def remote(src, dst, device):
        slot = count[0]
        count[0] += 1
        copy = pltpu.make_async_remote_copy(
            src_ref=src, dst_ref=dst, send_sem=send_sem.at[slot], recv_sem=recv_sem.at[slot],
            device_id=device, device_id_type=MESH)
        copy.start()
        return copy

    def correlate():
        rows = own + 16
        for a in range(4):
            r4[:, 512 * a:512 * a + 512] = r[8 * a:8 * a + rows, :]
        acc = None
        for a in range(4):
            d = lax.dot_general(r4[:, 512 * a:512 * a + 512], w_ref[512 * a:512 * a + 512, :], NT,
                                preferred_element_type=F32)
            acc = d if acc is None else acc + d
        q[...] = acc
        s = q[0:own + 8, 0:LANES]
        for b in range(1, 4):
            s = s + q[2 * b:2 * b + own + 8, LANES * b:LANES * b + LANES]
        return s[0:own, 0:FACTORS] + s[1:own + 1, FACTORS:2 * FACTORS]

    def stack():
        for j in range(LAGS // 2):
            hst[:, LANES * j:LANES * j + LANES] = (
                df[HALO - 2 * j:HALO - 2 * j + own + HALO, :].astype(BF16))

    def convolve():
        rows = own + HALO
        r[0:rows, :] = jnp.dot(hst[...], w_ref[...], preferred_element_type=F32).astype(BF16)
        tail = r[own:rows, :]
        r[own:rows, :] = jnp.where(last, jnp.zeros_like(tail), tail)

    def put_field(field):
        df[HALO:HALO + own, 0:FACTORS] = field
        df[HALO + 1:HALO + own + 1, FACTORS:2 * FACTORS] = field
        hi = field.astype(BF16)
        lo = (field - hi.astype(F32)).astype(BF16)
        fa[:, 0:FACTORS] = hi
        fa[:, FACTORS:2 * FACTORS] = lo

    def put_halos(it):
        from_left = halo_l[it]
        from_left = jnp.where(first, jnp.zeros_like(from_left), from_left)
        from_right = halo_r[it]
        df[0:HALO, 0:FACTORS] = from_left
        df[1:HALO + 1, FACTORS:2 * FACTORS] = from_left
        df[HALO + own:own + 2 * HALO, 0:FACTORS] = from_right
        df[HALO + own + 1:own + 2 * HALO, FACTORS:2 * FACTORS] = from_right[0:HALO - 1]

    def send_halos(it, field):
        halo_src[it, 0] = field[0:HALO]
        halo_src[it, 1] = field[own - HALO:own]
        return [remote(halo_src.at[it, 0], halo_r.at[it], left),
                remote(halo_src.at[it, 1], halo_l.at[it], right)]

    row_id = lax.broadcasted_iota(jnp.int32, (FACTORS, FACTORS), 0)
    col_id = lax.broadcasted_iota(jnp.int32, (FACTORS, FACTORS), 1)
    off_mask = jnp.where(row_id == col_id, 0.0, penalty_weight / total).astype(F32)

    mine = pl.ds(pl.multiple_of(y * own, own), own)
    df[0:8, :] = jnp.zeros((8, 2 * FACTORS), F32)

    src[...] = jnp.zeros_like(src)
    src[:, 0:blocks] = m_ref[...].astype(F32).T.astype(BF16)
    pieces = [remote(src, got.at[core, y, x, z], dev) for dev in along_z]
    got[core, y, x, z] = src[...]
    sent = list(pieces)
    data = []
    for d in range(1, ny):
        there = (y + d) % ny
        columns = pl.ds(pl.multiple_of(there * own, own), own)
        data.append(remote(x_ref.at[:, columns], tiles.at[y], along_y[d - 1]))
    tiles[y] = x_ref[:, mine]
    sent += data

    def gram_start(it):
        gg = lax.dot_general(fa[...], fa[...], TN, preferred_element_type=F32)
        gram = (gg[0:FACTORS, 0:FACTORS] + gg[0:FACTORS, FACTORS:] + gg[FACTORS:, 0:FACTORS]
                + gg[FACTORS:, FACTORS:])
        packed = jnp.concatenate([gram[0:32], gram[32:64]], axis=1)
        gsrc[it, 0] = packed[0:16]
        gsrc[it, 1] = packed[16:32]
        return remote(gsrc.at[it, 1 - core], cbuf.at[it], other)

    def gram_across(it, c0):
        c0.wait_recv()
        part[it, 0] = gsrc[it, core] + cbuf[it]
        return [remote(part.at[it, 0], xybuf.at[it, d], dev) for d, dev in enumerate(across)]

    def gram_along(it, cx):
        acc = part[it, 0]
        for d, c in enumerate(cx):
            c.wait_recv()
            acc = acc + xybuf[it, d]
        part[it, 1] = acc
        return [remote(part.at[it, 1], zbuf.at[it, d], dev) for d, dev in enumerate(along_z)]

    def gram_back(it, cz):
        acc = part[it, 1]
        for d, c in enumerate(cz):
            c.wait_recv()
            acc = acc + zbuf[it, d]
        part[it, 2] = acc
        return remote(part.at[it, 2], gtot.at[it], other)

    def gram_end(it, c1):
        c1.wait_recv()
        ours, theirs = part[it, 2], gtot[it]
        low = jnp.where(core == 0, ours, theirs)
        high = jnp.where(core == 0, theirs, ours)
        packed = jnp.concatenate([low, high], axis=0)
        return jnp.concatenate([packed[:, 0:FACTORS], packed[:, FACTORS:]], axis=0) * off_mask

    def update(off, denom):
        off_hi = off.astype(BF16)
        off_lo = (off - off_hi.astype(F32)).astype(BF16)
        penalty = (jnp.dot(fa[...], jnp.concatenate([off_hi, off_hi], axis=0), preferred_element_type=F32)
                   + jnp.dot(fa[:, 0:FACTORS], off_lo, preferred_element_type=F32))
        return df[HALO:HALO + own, 0:FACTORS] * num[...] / (denom + penalty)

    field = h_ref[:, mine].T
    halos = send_halos(0, field)
    put_field(field)
    c0 = gram_start(0)
    cx = gram_across(0, c0)

    def to_partner(block):
        sent.append(remote(block, block, other))
        return sent[-1]

    for c in pieces:
        c.wait_recv()
    line = got.at[core, y, x]
    partner = [to_partner(line)]
    from_x = [remote(line, line, dev) for dev in along_x]
    from_y = [remote(line, line, dev) for dev in along_y]
    sent += from_x + from_y

    r[...] = jnp.zeros_like(r)
    for c in data:
        c.wait_recv()
    for c in range(ny):
        r[0:own, LANES * c:LANES * c + blocks] = tiles[c].astype(F32).T.astype(BF16)
    rim_src[...] = r[0:HALO, :]
    rims = [remote(rim_src, rim, left)]
    sent += rims

    cz = gram_along(0, cx)
    low_half, high_half = pl.ds(0, 16), pl.ds(16, 16)
    later = []
    for d in range(1, ny):
        from_y[d - 1].wait_recv()
        block = got.at[core, (y + ny - d) % ny, x]
        half = block.at[:, low_half, :]
        on = [remote(half, half, dev) for dev in along_x]
        later += [(c, got.at[core, (y + ny - d) % ny, (x + NX - e - 1) % NX].at[:, low_half, :])
                  for e, c in enumerate(on)]
        partner.append(to_partner(block))
    for d in range(1, NX):
        from_x[d - 1].wait_recv()
        block = got.at[core, y, (x + NX - d) % NX]
        half = block.at[:, high_half, :]
        on = [remote(half, half, dev) for dev in along_y]
        later += [(c, got.at[core, (y + ny - e - 1) % ny, (x + NX - d) % NX].at[:, high_half, :])
                  for e, c in enumerate(on)]
        partner.append(to_partner(block))
    c1 = gram_back(0, cz)
    for c in halos:
        c.wait_recv()
    put_halos(0)
    stack()
    for c in rims:
        c.wait_recv()
    tail = rim[...]
    r[own:own + HALO, :] = jnp.where(last, jnp.zeros_like(tail), tail)
    off = gram_end(0, c1)
    for c, half in later:
        c.wait_recv()
        partner.append(to_partner(half))
    sent += [c for c, _ in later]

    def spread(cc):
        def one(i, _):
            for xx in range(NX):
                for yy in range(ny):
                    wf[yy, pl.ds((i * NX + xx) * NC + cc, LAGS, stride=FACTORS), :] = (
                        got[cc, yy, xx, i].astype(F32))
            return 0

        lax.fori_loop(0, nz, one, 0)

    spread(core)
    for c in partner:
        c.wait_recv()
    spread(1 - core)

    def narrow(i, _):
        rows = pl.ds(pl.multiple_of(i * LANES, LANES), LANES)
        for yy in range(ny):
            w_ref[rows, LANES * yy:LANES * yy + LANES] = wf[yy, rows, :].astype(BF16)
        return 0

    lax.fori_loop(0, LAGS * FACTORS // LANES, narrow, 0)
    num[...] = correlate()
    convolve()
    denom = correlate()
    field = update(off, denom)
    sent += halos + [c0, c1] + cx + cz

    for it in range(1, ITERS):
        halos = send_halos(it, field)
        put_field(field)
        c0 = gram_start(it)
        cx = gram_across(it, c0)
        for c in halos:
            c.wait_recv()
        put_halos(it)
        stack()
        convolve()
        cz = gram_along(it, cx)
        denom = correlate()
        c1 = gram_back(it, cz)
        off = gram_end(it, c1)
        field = update(off, denom)
        sent += halos + [c0, c1] + cx + cz

    fin[...] = field.T
    out_ref[:, mine] = fin[...]
    copies = [remote(fin, out_ref.at[:, mine], dev) for dev in along_y]
    for c in copies:
        c.wait_recv()
    for c in sent + copies:
        c.wait_send()


def on_device(data, motifs, loadings):
    ntm, ny = lax.axis_size("tm"), lax.axis_size("chan")
    blocks, steps = data.shape
    own = steps // ny
    nz = ntm // (NX * NC)
    V = pl.BlockSpec(memory_space=pltpu.VMEM)
    copies = ITERS * (4 + NX * ny - 1 + nz - 1) + 120
    vm = pltpu.VMEM
    return pl.pallas_call(
        functools.partial(kernel, nz, ny, float(steps * ntm)),
        out_shape=jax.ShapeDtypeStruct((FACTORS, steps), F32),
        in_specs=[V, V, V],
        out_specs=V,
        scratch_shapes=[
            vm((LAGS, LANES), BF16),
            vm((NC, ny, NX, nz, LAGS, LANES), BF16),
            vm((ny, LAGS * FACTORS, LANES), F32),
            vm((LAGS * FACTORS, ny * LANES), BF16),
            vm((ny, blocks, own), BF16),
            vm((HALO, ny * LANES), BF16),
            vm((HALO, ny * LANES), BF16),
            vm((own + 2 * HALO, 2 * FACTORS), F32),
            vm((own + HALO, LAGS * FACTORS), BF16),
            vm((own + HALO + 16, ny * LANES), BF16),
            vm((own + 16, 4 * ny * LANES), BF16),
            vm((own + 16, 4 * LANES), F32),
            vm((own, FACTORS), F32),
            vm((own, 2 * FACTORS), BF16),
            vm((ITERS, 2, HALO, FACTORS), F32),
            vm((ITERS, HALO, FACTORS), F32),
            vm((ITERS, HALO, FACTORS), F32),
            vm((ITERS, 2, 16, LANES), F32),
            vm((ITERS, 16, LANES), F32),
            vm((ITERS, 4, 16, LANES), F32),
            vm((ITERS, NX * ny - 1, 16, LANES), F32),
            vm((ITERS, nz - 1, 16, LANES), F32),
            vm((ITERS, 16, LANES), F32),
            vm((FACTORS, own), F32),
            pltpu.SemaphoreType.DMA((copies,)),
            pltpu.SemaphoreType.DMA((copies,)),
        ],
        compiler_params=pltpu.CompilerParams(collective_id=0, has_side_effects=True),
    )(motifs, data, loadings)


def solution(mesh):
    in_specs = (P("chan", "tm"), P("chan", "tm"), P(None, "tm"))
    out_specs = P(None, "tm")
    return jax.shard_map(
        on_device, mesh=mesh, in_specs=in_specs, out_specs=out_specs, check_vma=False
    )
```

```python
import functools

import jax
import jax.numpy as jnp
from jax import lax
from jax.experimental import pallas as pl
from jax.experimental.pallas import tpu as pltpu
from jax.sharding import PartitionSpec as P

FACTORS = 64
LAGS = 32
ITERS = 3
LANES = 128
HALO = LAGS
penalty_weight = 0.2

F32 = jnp.float32
BF16 = jnp.bfloat16
MESH = pl.DeviceIdType.MESH
NT = (((1,), (1,)), ((), ()))
TN = (((0,), (0,)), ((), ()))

NX = 4
NC = 2


def kernel(nz, ny, total, m_ref, x_ref, h_ref, out_ref, src, got, wf, w_ref, tiles, h_own, rim_src, rim,
           df, hst, r, r4, q, num, fa, halo_src, halo_l, halo_r, gsrc, cbuf, part, xybuf, zbuf, gtot,
           fin, send_sem, recv_sem, in_sem):
    blocks = m_ref.shape[1]
    own = h_ref.shape[1] // ny
    tm = lax.axis_index("tm")
    y = lax.axis_index("chan")
    core = tm % NC
    x = (tm // NC) % NX
    z = tm // (NC * NX)
    ntm = nz * NX * NC

    def at(zz, xx, cc, yy):
        return ((zz * NX + xx) * NC + cc, yy)

    spot = tm * ny + y
    right_spot = (spot + 1) % (ntm * ny)
    left_spot = (spot + ntm * ny - 1) % (ntm * ny)
    right = (right_spot // ny, right_spot % ny)
    left = (left_spot // ny, left_spot % ny)
    first = spot == 0
    last = spot == ntm * ny - 1

    other = at(z, x, 1 - core, y)
    along_x = [at(z, (x + d) % NX, core, y) for d in range(1, NX)]
    along_y = [at(z, x, core, (y + d) % ny) for d in range(1, ny)]
    across = [at(z, (x + d) % NX, core, (y + e) % ny) for d in range(NX) for e in range(ny) if d or e]
    along_z = [at((z + d) % nz, x, core, y) for d in range(1, nz)]

    mine = pl.ds(pl.multiple_of(y * own, own), own)
    h_in = pltpu.make_async_copy(h_ref.at[:, mine], h_own, in_sem.at[0])
    h_in.start()
    x_in = pltpu.make_async_copy(x_ref.at[:, mine], tiles.at[y], in_sem.at[1])
    x_in.start()

    barrier = pltpu.get_barrier_semaphore()
    everyone = [other, left, right] + across + along_z
    for device in everyone:
        pl.semaphore_signal(barrier, inc=1, device_id=device, device_id_type=MESH)
    src[...] = jnp.zeros_like(src)
    src[:, 0:blocks] = m_ref[...]
    df[0:8, :] = jnp.zeros((8, 2 * FACTORS), F32)
    pl.semaphore_wait(barrier, len(everyone))

    count = [0]

    def remote(src, dst, device, at_slot=None):
        slot = count[0]
        count[0] += 1
        copy = pltpu.make_async_remote_copy(
            src_ref=src, dst_ref=dst, send_sem=send_sem.at[slot],
            recv_sem=recv_sem.at[slot if at_slot is None else at_slot],
            device_id=device, device_id_type=MESH)
        copy.start()
        return copy

    def arrival(block, slot):
        pltpu.make_async_remote_copy(
            src_ref=block, dst_ref=block, send_sem=send_sem.at[slot], recv_sem=recv_sem.at[slot],
            device_id=other, device_id_type=MESH).wait_recv()

    def correlate():
        rows = own + 16
        for a in range(4):
            r4[:, 512 * a:512 * a + 512] = r[8 * a:8 * a + rows, :]
        acc = None
        for a in range(4):
            d = lax.dot_general(r4[:, 512 * a:512 * a + 512], w_ref[512 * a:512 * a + 512, :], NT,
                                preferred_element_type=F32)
            acc = d if acc is None else acc + d
        q[...] = acc
        s = q[0:own + 8, 0:LANES]
        for b in range(1, 4):
            s = s + q[2 * b:2 * b + own + 8, LANES * b:LANES * b + LANES]
        return s[0:own, 0:FACTORS] + s[1:own + 1, FACTORS:2 * FACTORS]

    def stack():
        for j in range(LAGS // 2):
            hst[:, LANES * j:LANES * j + LANES] = (
                df[HALO - 2 * j:HALO - 2 * j + own + HALO, :].astype(BF16))

    def convolve():
        rows = own + HALO
        r[0:rows, :] = jnp.dot(hst[...], w_ref[...], preferred_element_type=F32).astype(BF16)
        tail = r[own:rows, :]
        r[own:rows, :] = jnp.where(last, jnp.zeros_like(tail), tail)

    def put_field(field):
        df[HALO:HALO + own, 0:FACTORS] = field
        df[HALO + 1:HALO + own + 1, FACTORS:2 * FACTORS] = field

    def put_gram(field):
        hi = field.astype(BF16)
        lo = (field - hi.astype(F32)).astype(BF16)
        fa[:, 0:FACTORS] = hi
        fa[:, FACTORS:2 * FACTORS] = lo

    def put_halos(it):
        from_left = halo_l[it]
        from_left = jnp.where(first, jnp.zeros_like(from_left), from_left)
        from_right = halo_r[it]
        df[0:HALO, 0:FACTORS] = from_left
        df[1:HALO + 1, FACTORS:2 * FACTORS] = from_left
        df[HALO + own:own + 2 * HALO, 0:FACTORS] = from_right
        df[HALO + own + 1:own + 2 * HALO, FACTORS:2 * FACTORS] = from_right[0:HALO - 1]

    def send_halos(it, field):
        halo_src[it, 0] = field[0:HALO]
        halo_src[it, 1] = field[own - HALO:own]
        return [remote(halo_src.at[it, 0], halo_r.at[it], left),
                remote(halo_src.at[it, 1], halo_l.at[it], right)]

    row_id = lax.broadcasted_iota(jnp.int32, (FACTORS, FACTORS), 0)
    col_id = lax.broadcasted_iota(jnp.int32, (FACTORS, FACTORS), 1)
    off_mask = jnp.where(row_id == col_id, 0.0, penalty_weight / total).astype(F32)

    got[core, y, x, z] = src[...]
    pairs = nz // 2
    pair = z // 2
    base = count[0]
    count[0] += pairs
    piece = got.at[core, y, x, z]
    sent = [remote(src, piece, at(pair * 2 + 1 - z % 2, x, core, y), base)]
    for p in [1, pairs - 1] + list(range(2, pairs - 1)):
        for b in range(2):
            there = (pair + pairs - p) % pairs * 2 + b
            sent.append(remote(src, piece, at(there, x, core, y), base + p))
    data = []
    for d in range(1, ny):
        there = (y + d) % ny
        columns = pl.ds(pl.multiple_of(there * own, own), own)
        data.append(remote(x_ref.at[:, columns], tiles.at[y], along_y[d - 1]))
    sent += data

    def gram_start(it):
        gg = lax.dot_general(fa[...], fa[...], TN, preferred_element_type=F32)
        gram = (gg[0:FACTORS, 0:FACTORS] + gg[0:FACTORS, FACTORS:] + gg[FACTORS:, 0:FACTORS]
                + gg[FACTORS:, FACTORS:])
        packed = jnp.concatenate([gram[0:32], gram[32:64]], axis=1)
        gsrc[it, 0] = packed[0:16]
        gsrc[it, 1] = packed[16:32]
        return remote(gsrc.at[it, 1 - core], cbuf.at[it], other)

    def gram_across(it, c0):
        c0.wait_recv()
        part[it, 0] = gsrc[it, core] + cbuf[it]
        return [remote(part.at[it, 0], xybuf.at[it, d], dev) for d, dev in enumerate(across)]

    def gram_along(it, cx):
        acc = part[it, 0]
        for d, c in enumerate(cx):
            c.wait_recv()
            acc = acc + xybuf[it, d]
        part[it, 1] = acc
        return [remote(part.at[it, 1], zbuf.at[it, d], dev) for d, dev in enumerate(along_z)]

    def gram_back(it, cz):
        acc = part[it, 1]
        for d, c in enumerate(cz):
            c.wait_recv()
            acc = acc + zbuf[it, d]
        part[it, 2] = acc
        return remote(part.at[it, 2], gtot.at[it], other)

    def gram_end(it, c1):
        c1.wait_recv()
        ours, theirs = part[it, 2], gtot[it]
        low = jnp.where(core == 0, ours, theirs)
        high = jnp.where(core == 0, theirs, ours)
        packed = jnp.concatenate([low, high], axis=0)
        return jnp.concatenate([packed[:, 0:FACTORS], packed[:, FACTORS:]], axis=0) * off_mask

    def update(off, denom):
        off_hi = off.astype(BF16)
        off_lo = (off - off_hi.astype(F32)).astype(BF16)
        penalty = (jnp.dot(fa[...], jnp.concatenate([off_hi, off_hi], axis=0), preferred_element_type=F32)
                   + jnp.dot(fa[:, 0:FACTORS], off_lo, preferred_element_type=F32))
        return df[HALO:HALO + own, 0:FACTORS] * num[...] / (denom + penalty)

    def to_partner(block):
        copy = remote(block, block, other)
        sent.append(copy)
        return copy

    def spread(cc, yy, xx):
        def one(i, _):
            k = (i * NX + xx) * NC + cc
            wf[yy, pl.ds(k, LAGS, stride=FACTORS), :] = got[cc, yy, xx, i].astype(F32)
            return 0

        lax.fori_loop(0, nz, one, 0, unroll=True)

    h_in.wait()
    field = h_own[...].T
    put_gram(field)
    c0 = gram_start(0)
    halos = send_halos(0, field)

    order = [0, 1, pairs - 1] + list(range(2, pairs - 1))
    low_half, high_half = pl.ds(0, 16), pl.ds(16, 16)

    def zs(p):
        return pl.ds((pair + p) % pairs * 2, 2)

    from_x, from_y = {}, {}
    for p in order:
        if p == 0:
            arrival(got.at[core, y, x, pair * 2 + 1 - z % 2], base)
        else:
            arrival(got.at[core, y, x, zs(p)], base + p)
        block = got.at[core, y, x, zs(p)]
        for d in (1, ny - 1, 2):
            from_y[p, d] = remote(block, block, along_y[d - 1])
        for d in (1, NX - 1, 2):
            from_x[p, d] = remote(block, block, along_x[d - 1])
        if p == 0:
            cx = gram_across(0, c0)
    partner = [(to_partner(got.at[core, y, x]), y, x)]
    sent += list(from_x.values()) + list(from_y.values())
    put_field(field)

    r[...] = jnp.zeros_like(r)
    x_in.wait()
    for c in data:
        c.wait_recv()
    for c in range(ny):
        r[0:own, LANES * c:LANES * c + blocks] = tiles[c].astype(F32).T.astype(BF16)
    rim_src[...] = r[0:HALO, :]
    rims = [remote(rim_src, rim, left)]
    sent += rims

    later = {}
    for p in order:
        for d in (1, 3, 2):
            yy, xx = (y + ny - d) % ny, (x + NX - d) % NX
            from_y[p, d].wait_recv()
            half = got.at[core, yy, x, zs(p), low_half]
            for e in (1, 3, 2):
                later.setdefault((d, e), []).append(remote(half, half, along_x[e - 1]))
            from_x[p, d].wait_recv()
            half = got.at[core, y, xx, zs(p), high_half]
            for e in (1, 3, 2):
                later.setdefault((e, d), []).append(remote(half, half, along_y[e - 1]))
        if p == order[0]:
            cz = gram_along(0, cx)
    lines = []
    for d in range(1, NX):
        yy, xx = (y + ny - d) % ny, (x + NX - d) % NX
        lines += [(yy, x), (y, xx)]
    partner += [(to_partner(got.at[core, yy, xx]), yy, xx) for yy, xx in lines]
    c1 = gram_back(0, cz)
    for c in halos:
        c.wait_recv()
    put_halos(0)
    stack()
    for c in rims:
        c.wait_recv()
    tail = rim[...]
    r[own:own + HALO, :] = jnp.where(last, jnp.zeros_like(tail), tail)
    spread(core, y, x)
    for yy, xx in lines:
        spread(core, yy, xx)
    early, partner = partner, []
    for c, yy, xx in early:
        c.wait_recv()
        spread(1 - core, yy, xx)
    for (d, e), copies in later.items():
        for c in copies:
            c.wait_recv()
        yy, xx = (y + ny - d) % ny, (x + NX - e) % NX
        partner.append((to_partner(got.at[core, yy, xx]), yy, xx))
        spread(core, yy, xx)
        sent += copies
    off = gram_end(0, c1)
    for c, yy, xx in partner:
        c.wait_recv()
        spread(1 - core, yy, xx)

    def narrow(i, _):
        rows = pl.ds(pl.multiple_of(i * LANES, LANES), LANES)
        for yy in range(ny):
            w_ref[rows, LANES * yy:LANES * yy + LANES] = wf[yy, rows, :].astype(BF16)
        return 0

    lax.fori_loop(0, LAGS * FACTORS // LANES, narrow, 0)
    num[...] = correlate()
    convolve()
    denom = correlate()
    field = update(off, denom)
    sent += halos + [c0, c1] + cx + cz

    for it in range(1, ITERS):
        put_gram(field)
        c0 = gram_start(it)
        halos = send_halos(it, field)
        put_field(field)
        cx = gram_across(it, c0)
        for c in halos:
            c.wait_recv()
        put_halos(it)
        stack()
        convolve()
        cz = gram_along(it, cx)
        denom = correlate()
        c1 = gram_back(it, cz)
        off = gram_end(it, c1)
        field = update(off, denom)
        sent += halos + [c0, c1] + cx + cz

    fin[...] = field.T
    out_ref[:, mine] = fin[...]
    copies = [remote(fin, out_ref.at[:, mine], dev) for dev in along_y]
    for c in copies:
        c.wait_recv()
    for c in sent + copies:
        c.wait_send()


def on_device(data, motifs, loadings):
    ntm, ny = lax.axis_size("tm"), lax.axis_size("chan")
    blocks, steps = data.shape
    own = steps // ny
    nz = ntm // (NX * NC)
    V = pl.BlockSpec(memory_space=pltpu.VMEM)
    A = pl.BlockSpec(memory_space=pl.ANY)
    copies = ITERS * (4 + NX * ny - 1 + nz - 1) + 160
    vm = pltpu.VMEM
    return pl.pallas_call(
        functools.partial(kernel, nz, ny, float(steps * ntm)),
        out_shape=jax.ShapeDtypeStruct((FACTORS, steps), F32),
        in_specs=[V, A, A],
        out_specs=V,
        scratch_shapes=[
            vm((LAGS, LANES), BF16),
            vm((NC, ny, NX, nz, LAGS, LANES), BF16),
            vm((ny, LAGS * FACTORS, LANES), F32),
            vm((LAGS * FACTORS, ny * LANES), BF16),
            vm((ny, blocks, own), BF16),
            vm((FACTORS, own), F32),
            vm((HALO, ny * LANES), BF16),
            vm((HALO, ny * LANES), BF16),
            vm((own + 2 * HALO, 2 * FACTORS), F32),
            vm((own + HALO, LAGS * FACTORS), BF16),
            vm((own + HALO + 16, ny * LANES), BF16),
            vm((own + 16, 4 * ny * LANES), BF16),
            vm((own + 16, 4 * LANES), F32),
            vm((own, FACTORS), F32),
            vm((own, 2 * FACTORS), BF16),
            vm((ITERS, 2, HALO, FACTORS), F32),
            vm((ITERS, HALO, FACTORS), F32),
            vm((ITERS, HALO, FACTORS), F32),
            vm((ITERS, 2, 16, LANES), F32),
            vm((ITERS, 16, LANES), F32),
            vm((ITERS, 4, 16, LANES), F32),
            vm((ITERS, NX * ny - 1, 16, LANES), F32),
            vm((ITERS, nz - 1, 16, LANES), F32),
            vm((ITERS, 16, LANES), F32),
            vm((FACTORS, own), F32),
            pltpu.SemaphoreType.DMA((copies,)),
            pltpu.SemaphoreType.DMA((copies,)),
            pltpu.SemaphoreType.DMA((2,)),
        ],
        compiler_params=pltpu.CompilerParams(collective_id=0, has_side_effects=True),
    )(motifs.T, data, loadings)


def solution(mesh):
    in_specs = (P("chan", "tm"), P("chan", "tm"), P(None, "tm"))
    out_specs = P(None, "tm")
    return jax.shard_map(
        on_device, mesh=mesh, in_specs=in_specs, out_specs=out_specs, check_vma=False
    )
```

```python
import functools

import jax
import jax.numpy as jnp
from jax import lax
from jax.experimental import pallas as pl
from jax.experimental.pallas import tpu as pltpu
from jax.sharding import PartitionSpec as P

FACTORS = 64
LAGS = 32
ITERS = 3
LANES = 128
HALO = LAGS
penalty_weight = 0.2

F32 = jnp.float32
BF16 = jnp.bfloat16
MESH = pl.DeviceIdType.MESH
NT = (((1,), (1,)), ((), ()))
TN = (((0,), (0,)), ((), ()))

NX = 4
NC = 2


def kernel(nz, ny, total, m_ref, x_ref, h_ref, out_ref, src, got, wf, w_ref, tiles, h_own, rim_src, rim,
           df, hst, r, r4, q, num, fa, halo_src, halo_l, halo_r, gsrc, cbuf, part, xybuf, zbuf, gtot,
           all_n, all_f, all_d, all_a, fb, send_sem, recv_sem, in_sem):
    blocks = m_ref.shape[1]
    own = h_ref.shape[1] // ny
    tm = lax.axis_index("tm")
    y = lax.axis_index("chan")
    core = tm % NC
    x = (tm // NC) % NX
    z = tm // (NC * NX)
    ntm = nz * NX * NC

    def at(zz, xx, cc, yy):
        return ((zz * NX + xx) * NC + cc, yy)

    spot = tm * ny + y
    right_spot = (spot + 1) % (ntm * ny)
    left_spot = (spot + ntm * ny - 1) % (ntm * ny)
    right = (right_spot // ny, right_spot % ny)
    left = (left_spot // ny, left_spot % ny)
    first = spot == 0
    last = spot == ntm * ny - 1

    other = at(z, x, 1 - core, y)
    along_x = [at(z, (x + d) % NX, core, y) for d in range(1, NX)]
    along_y = [at(z, x, core, (y + d) % ny) for d in range(1, ny)]
    across = [at(z, (x + d) % NX, core, (y + e) % ny) for d in range(NX) for e in range(ny) if d or e]
    along_z = [at((z + d) % nz, x, core, y) for d in range(1, nz)]

    mine = pl.ds(pl.multiple_of(y * own, own), own)
    h_in = pltpu.make_async_copy(h_ref.at[:, mine], h_own, in_sem.at[0])
    h_in.start()
    x_in = pltpu.make_async_copy(x_ref.at[:, mine], tiles.at[y], in_sem.at[1])
    x_in.start()

    barrier = pltpu.get_barrier_semaphore()
    everyone = [other, left, right] + across + along_z
    for device in everyone:
        pl.semaphore_signal(barrier, inc=1, device_id=device, device_id_type=MESH)
    src[...] = jnp.zeros_like(src)
    src[:, 0:blocks] = m_ref[...]
    df[0:8, :] = jnp.zeros((8, 2 * FACTORS), F32)
    pl.semaphore_wait(barrier, len(everyone))

    count = [0]

    def remote(src, dst, device, at_slot=None):
        slot = count[0]
        count[0] += 1
        copy = pltpu.make_async_remote_copy(
            src_ref=src, dst_ref=dst, send_sem=send_sem.at[slot],
            recv_sem=recv_sem.at[slot if at_slot is None else at_slot],
            device_id=device, device_id_type=MESH)
        copy.start()
        return copy

    def arrival(block, slot):
        pltpu.make_async_remote_copy(
            src_ref=block, dst_ref=block, send_sem=send_sem.at[slot], recv_sem=recv_sem.at[slot],
            device_id=other, device_id_type=MESH).wait_recv()

    def correlate():
        rows = own + 16
        for a in range(4):
            r4[:, 512 * a:512 * a + 512] = r[8 * a:8 * a + rows, :]
        acc = None
        for a in range(4):
            d = lax.dot_general(r4[:, 512 * a:512 * a + 512], w_ref[512 * a:512 * a + 512, :], NT,
                                preferred_element_type=F32)
            acc = d if acc is None else acc + d
        q[...] = acc
        s = q[0:own + 8, 0:LANES]
        for b in range(1, 4):
            s = s + q[2 * b:2 * b + own + 8, LANES * b:LANES * b + LANES]
        return s[0:own, 0:FACTORS] + s[1:own + 1, FACTORS:2 * FACTORS]

    def stack():
        for j in range(LAGS // 2):
            hst[:, LANES * j:LANES * j + LANES] = (
                df[HALO - 2 * j:HALO - 2 * j + own + HALO, :].astype(BF16))

    def convolve():
        rows = own + HALO
        r[0:rows, :] = jnp.dot(hst[...], w_ref[...], preferred_element_type=F32).astype(BF16)
        tail = r[own:rows, :]
        r[own:rows, :] = jnp.where(last, jnp.zeros_like(tail), tail)

    def put_field(field):
        df[HALO:HALO + own, 0:FACTORS] = field
        df[HALO + 1:HALO + own + 1, FACTORS:2 * FACTORS] = field

    def put_gram(field):
        hi = field.astype(BF16)
        lo = (field - hi.astype(F32)).astype(BF16)
        fa[:, 0:FACTORS] = hi
        fa[:, FACTORS:2 * FACTORS] = lo

    def put_halos(it):
        from_left = halo_l[it]
        from_left = jnp.where(first, jnp.zeros_like(from_left), from_left)
        from_right = halo_r[it]
        df[0:HALO, 0:FACTORS] = from_left
        df[1:HALO + 1, FACTORS:2 * FACTORS] = from_left
        df[HALO + own:own + 2 * HALO, 0:FACTORS] = from_right
        df[HALO + own + 1:own + 2 * HALO, FACTORS:2 * FACTORS] = from_right[0:HALO - 1]

    def send_halos(it, field):
        halo_src[it, 0] = field[0:HALO]
        halo_src[it, 1] = field[own - HALO:own]
        return [remote(halo_src.at[it, 0], halo_r.at[it], left),
                remote(halo_src.at[it, 1], halo_l.at[it], right)]

    row_id = lax.broadcasted_iota(jnp.int32, (FACTORS, FACTORS), 0)
    col_id = lax.broadcasted_iota(jnp.int32, (FACTORS, FACTORS), 1)
    off_mask = jnp.where(row_id == col_id, 0.0, penalty_weight / total).astype(F32)

    got[core, y, x, z] = src[...]
    pairs = nz // 2
    pair = z // 2
    base = count[0]
    count[0] += pairs
    piece = got.at[core, y, x, z]
    sent = [remote(src, piece, at(pair * 2 + 1 - z % 2, x, core, y), base)]
    for p in [1, pairs - 1] + list(range(2, pairs - 1)):
        for b in range(2):
            there = (pair + pairs - p) % pairs * 2 + b
            sent.append(remote(src, piece, at(there, x, core, y), base + p))
    data = []
    for d in range(1, ny):
        there = (y + d) % ny
        columns = pl.ds(pl.multiple_of(there * own, own), own)
        data.append(remote(x_ref.at[:, columns], tiles.at[y], along_y[d - 1]))
    sent += data

    def gram_start(it):
        gg = lax.dot_general(fa[...], fa[...], TN, preferred_element_type=F32)
        gram = (gg[0:FACTORS, 0:FACTORS] + gg[0:FACTORS, FACTORS:] + gg[FACTORS:, 0:FACTORS]
                + gg[FACTORS:, FACTORS:])
        packed = jnp.concatenate([gram[0:32], gram[32:64]], axis=1)
        gsrc[it, 0] = packed[0:16]
        gsrc[it, 1] = packed[16:32]
        return remote(gsrc.at[it, 1 - core], cbuf.at[it], other)

    def gram_across(it, c0):
        c0.wait_recv()
        spot = x * ny + y
        xybuf[it, spot] = gsrc[it, core] + cbuf[it]
        return [remote(xybuf.at[it, spot], xybuf.at[it, spot], dev) for dev in across]

    def gram_along(it, cx):
        for c in cx:
            c.wait_recv()
        zbuf[it, z] = sum(xybuf[it, i] for i in range(NX * ny))
        return [remote(zbuf.at[it, z], zbuf.at[it, z], dev) for dev in along_z]

    def gram_back(it, cz):
        for c in cz:
            c.wait_recv()
        part[it] = sum(zbuf[it, i] for i in range(nz))
        return remote(part.at[it], gtot.at[it], other)

    def gram_end(it, c1):
        c1.wait_recv()
        ours, theirs = part[it], gtot[it]
        low = jnp.where(core == 0, ours, theirs)
        high = jnp.where(core == 0, theirs, ours)
        packed = jnp.concatenate([low, high], axis=0)
        return jnp.concatenate([packed[:, 0:FACTORS], packed[:, FACTORS:]], axis=0) * off_mask

    def update(off, denom):
        off_hi = off.astype(BF16)
        off_lo = (off - off_hi.astype(F32)).astype(BF16)
        penalty = (jnp.dot(fa[...], jnp.concatenate([off_hi, off_hi], axis=0), preferred_element_type=F32)
                   + jnp.dot(fa[:, 0:FACTORS], off_lo, preferred_element_type=F32))
        return df[HALO:HALO + own, 0:FACTORS] * num[...] / (denom + penalty)

    def to_partner(block):
        copy = remote(block, block, other)
        sent.append(copy)
        return copy

    def spread(cc, yy, xx):
        def one(i, _):
            k = (i * NX + xx) * NC + cc
            wf[yy, pl.ds(k, LAGS, stride=FACTORS), :] = got[cc, yy, xx, i].astype(F32)
            return 0

        lax.fori_loop(0, nz, one, 0, unroll=True)

    h_in.wait()
    field = h_own[...].T
    put_gram(field)
    c0 = gram_start(0)
    halos = send_halos(0, field)

    order = [0, 1, pairs - 1] + list(range(2, pairs - 1))
    low_half, high_half = pl.ds(0, 16), pl.ds(16, 16)

    def zs(p):
        return pl.ds((pair + p) % pairs * 2, 2)

    from_x, from_y = {}, {}
    for p in order:
        if p == 0:
            arrival(got.at[core, y, x, pair * 2 + 1 - z % 2], base)
        else:
            arrival(got.at[core, y, x, zs(p)], base + p)
        block = got.at[core, y, x, zs(p)]
        for d in (1, ny - 1, 2):
            from_y[p, d] = remote(block, block, along_y[d - 1])
        for d in (1, NX - 1, 2):
            from_x[p, d] = remote(block, block, along_x[d - 1])
        if p == 0:
            cx = gram_across(0, c0)
    partner = [(to_partner(got.at[core, y, x]), y, x)]
    sent += list(from_x.values()) + list(from_y.values())
    put_field(field)

    r[...] = jnp.zeros_like(r)
    x_in.wait()
    for c in data:
        c.wait_recv()
    for c in range(ny):
        r[0:own, LANES * c:LANES * c + blocks] = tiles[c].astype(F32).T.astype(BF16)
    rim_src[...] = r[0:HALO, :]
    rims = [remote(rim_src, rim, left)]
    sent += rims

    later = {}
    for p in order:
        for d in (1, 3, 2):
            yy, xx = (y + ny - d) % ny, (x + NX - d) % NX
            from_y[p, d].wait_recv()
            half = got.at[core, yy, x, zs(p)] if p in order[:2] else got.at[core, yy, x, zs(p), low_half]
            for e in (1, 3, 2):
                later.setdefault((d, e), []).append(remote(half, half, along_x[e - 1]))
            from_x[p, d].wait_recv()
            if p in order[:2]:
                continue
            half = got.at[core, y, xx, zs(p), high_half]
            for e in (1, 3, 2):
                later.setdefault((e, d), []).append(remote(half, half, along_y[e - 1]))
        if p == order[0]:
            cz = gram_along(0, cx)
    lines = []
    for d in range(1, NX):
        yy, xx = (y + ny - d) % ny, (x + NX - d) % NX
        lines += [(yy, x), (y, xx)]
    partner += [(to_partner(got.at[core, yy, xx]), yy, xx) for yy, xx in lines]
    c1 = gram_back(0, cz)
    for c in halos:
        c.wait_recv()
    put_halos(0)
    stack()
    for c in rims:
        c.wait_recv()
    tail = rim[...]
    r[own:own + HALO, :] = jnp.where(last, jnp.zeros_like(tail), tail)
    spread(core, y, x)
    for yy, xx in lines:
        spread(core, yy, xx)
    early, partner = partner, []
    for c, yy, xx in early:
        c.wait_recv()
        spread(1 - core, yy, xx)
    for (d, e), copies in later.items():
        for c in copies:
            c.wait_recv()
        yy, xx = (y + ny - d) % ny, (x + NX - e) % NX
        partner.append((to_partner(got.at[core, yy, xx]), yy, xx))
        spread(core, yy, xx)
        sent += copies
    off = gram_end(0, c1)
    for c, yy, xx in partner:
        c.wait_recv()
        spread(1 - core, yy, xx)

    def narrow(i, _):
        rows = pl.ds(pl.multiple_of(i * LANES, LANES), LANES)
        for yy in range(ny):
            w_ref[rows, LANES * yy:LANES * yy + LANES] = wf[yy, rows, :].astype(BF16)
        return 0

    lax.fori_loop(0, LAGS * FACTORS // LANES, narrow, 0)
    num[...] = correlate()
    convolve()
    denom = correlate()
    field = update(off, denom)
    sent += halos + [c0, c1] + cx + cz

    def to_all_blocks(value, everyone_has):
        everyone_has[y] = value.T
        copies = [remote(everyone_has.at[y], everyone_has.at[y], dev) for dev in along_y]
        sent.extend(copies)
        return copies

    for it in range(1, ITERS):
        put_gram(field)
        c0 = gram_start(it)
        halos = send_halos(it, field)
        put_field(field)
        cx = gram_across(it, c0)
        if it == ITERS - 1:
            f_in = to_all_blocks(field, all_f)
        for c in halos:
            c.wait_recv()
        put_halos(it)
        stack()
        convolve()
        if it < ITERS - 1:
            cz = gram_along(it, cx)
        denom = correlate()
        if it == ITERS - 1:
            d_in = to_all_blocks(denom, all_d)
            cz = gram_along(it, cx)
            for c in n_in + f_in:
                c.wait_recv()
            for yy in range(ny):
                f = all_f[yy]
                hi = f.astype(BF16)
                fb[yy, 0:FACTORS, :] = hi
                fb[yy, FACTORS:2 * FACTORS, :] = (f - hi.astype(F32)).astype(BF16)
                all_a[yy] = f * all_n[yy]
        elif it == 1:
            n_in = to_all_blocks(num[...], all_n)
        c1 = gram_back(it, cz)
        off = gram_end(it, c1)
        if it < ITERS - 1:
            field = update(off, denom)
        sent += halos + [c0, c1] + cx + cz

    off_hi = off.astype(BF16)
    off_lo = (off - off_hi.astype(F32)).astype(BF16)
    twice = jnp.concatenate([off_hi, off_hi], axis=1)
    for c in d_in:
        c.wait_recv()
    for yy in range(ny):
        penalty = (jnp.dot(twice, fb[yy], preferred_element_type=F32)
                   + jnp.dot(off_lo, fb[yy, 0:FACTORS, :], preferred_element_type=F32))
        out_ref[:, own * yy:own * yy + own] = all_a[yy] / (all_d[yy] + penalty)
    for c in sent:
        c.wait_send()


def on_device(data, motifs, loadings):
    ntm, ny = lax.axis_size("tm"), lax.axis_size("chan")
    blocks, steps = data.shape
    own = steps // ny
    nz = ntm // (NX * NC)
    V = pl.BlockSpec(memory_space=pltpu.VMEM)
    A = pl.BlockSpec(memory_space=pl.ANY)
    copies = ITERS * (4 + NX * ny - 1 + nz - 1) + 160
    vm = pltpu.VMEM
    return pl.pallas_call(
        functools.partial(kernel, nz, ny, float(steps * ntm)),
        out_shape=jax.ShapeDtypeStruct((FACTORS, steps), F32),
        in_specs=[V, A, A],
        out_specs=V,
        scratch_shapes=[
            vm((LAGS, LANES), BF16),
            vm((NC, ny, NX, nz, LAGS, LANES), BF16),
            vm((ny, LAGS * FACTORS, LANES), F32),
            vm((LAGS * FACTORS, ny * LANES), BF16),
            vm((ny, blocks, own), BF16),
            vm((FACTORS, own), F32),
            vm((HALO, ny * LANES), BF16),
            vm((HALO, ny * LANES), BF16),
            vm((own + 2 * HALO, 2 * FACTORS), F32),
            vm((own + HALO, LAGS * FACTORS), BF16),
            vm((own + HALO + 16, ny * LANES), BF16),
            vm((own + 16, 4 * ny * LANES), BF16),
            vm((own + 16, 4 * LANES), F32),
            vm((own, FACTORS), F32),
            vm((own, 2 * FACTORS), BF16),
            vm((ITERS, 2, HALO, FACTORS), F32),
            vm((ITERS, HALO, FACTORS), F32),
            vm((ITERS, HALO, FACTORS), F32),
            vm((ITERS, 2, 16, LANES), F32),
            vm((ITERS, 16, LANES), F32),
            vm((ITERS, 16, LANES), F32),
            vm((ITERS, NX * ny, 16, LANES), F32),
            vm((ITERS, nz, 16, LANES), F32),
            vm((ITERS, 16, LANES), F32),
            vm((ny, FACTORS, own), F32),
            vm((ny, FACTORS, own), F32),
            vm((ny, FACTORS, own), F32),
            vm((ny, FACTORS, own), F32),
            vm((ny, 2 * FACTORS, own), BF16),
            pltpu.SemaphoreType.DMA((copies,)),
            pltpu.SemaphoreType.DMA((copies,)),
            pltpu.SemaphoreType.DMA((2,)),
        ],
        compiler_params=pltpu.CompilerParams(collective_id=0, has_side_effects=True),
    )(motifs.T, data, loadings)


def solution(mesh):
    in_specs = (P("chan", "tm"), P("chan", "tm"), P(None, "tm"))
    out_specs = P(None, "tm")
    return jax.shard_map(
        on_device, mesh=mesh, in_specs=in_specs, out_specs=out_specs, check_vma=False
    )
```

```python
import functools

import jax
import jax.numpy as jnp
from jax import lax
from jax.experimental import pallas as pl
from jax.experimental.pallas import tpu as pltpu
from jax.sharding import PartitionSpec as P

FACTORS = 64
LAGS = 32
ITERS = 3
LANES = 128
HALO = LAGS
SLOTS = 84
penalty_weight = 0.2

F32 = jnp.float32
BF16 = jnp.bfloat16
MESH = pl.DeviceIdType.MESH
NT = (((1,), (1,)), ((), ()))
TN = (((0,), (0,)), ((), ()))

NX = 4
NC = 2


def kernel(nz, ny, total, m_ref, x_ref, h_ref, out_ref, src, got, wf, w_ref, tiles, h_own, rim_src, rim,
           df, hst, r, r4, q, num, fa, halo_src, halo_l, halo_r, gsrc, cbuf, part, xybuf, zbuf, gtot,
           all_n, all_f, all_d, all_a, fb, sem, in_sem):
    blocks = m_ref.shape[1]
    own = h_ref.shape[1] // ny
    tm = lax.axis_index("tm")
    y = lax.axis_index("chan")
    core = tm % NC
    x = (tm // NC) % NX
    z = tm // (NC * NX)
    ntm = nz * NX * NC

    def at(zz, xx, cc, yy):
        return ((zz * NX + xx) * NC + cc, yy)

    spot = tm * ny + y
    right_spot = (spot + 1) % (ntm * ny)
    left_spot = (spot + ntm * ny - 1) % (ntm * ny)
    right = (right_spot // ny, right_spot % ny)
    left = (left_spot // ny, left_spot % ny)
    first = spot == 0
    last = spot == ntm * ny - 1

    other = at(z, x, 1 - core, y)
    along_x = [at(z, (x + d) % NX, core, y) for d in range(1, NX)]
    along_y = [at(z, x, core, (y + d) % ny) for d in range(1, ny)]
    across = [at(z, (x + d) % NX, core, (y + e) % ny) for d in range(NX) for e in range(ny) if d or e]
    along_z = [at((z + d) % nz, x, core, y) for d in range(1, nz)]

    mine = pl.ds(pl.multiple_of(y * own, own), own)
    h_in = pltpu.make_async_copy(h_ref.at[:, mine], h_own, in_sem.at[0])
    h_in.start()
    x_in = pltpu.make_async_copy(x_ref.at[:, mine], tiles.at[y], in_sem.at[1])
    x_in.start()

    barrier = pltpu.get_barrier_semaphore()
    everyone = [other, left, right] + across + along_z
    for device in everyone:
        pl.semaphore_signal(barrier, inc=1, device_id=device, device_id_type=MESH)
    src[...] = jnp.zeros_like(src)
    src[:, 0:blocks] = m_ref[...]
    df[0:8, :] = jnp.zeros((8, 2 * FACTORS), F32)
    pl.semaphore_wait(barrier, len(everyone))

    count = [0]

    def slot():
        count[0] += 1
        return count[0] - 1

    def copy_of(src, dst, device, send, recv):
        return pltpu.make_async_remote_copy(
            src_ref=src, dst_ref=dst, send_sem=sem.at[send], recv_sem=sem.at[recv],
            device_id=device, device_id_type=MESH)

    def remote(src, dst, device, send, recv):
        copy_of(src, dst, device, send, recv).start()

    def arrival(block, recv):
        copy_of(block, block, other, recv, recv).wait_recv()

    def departure(block, send):
        copy_of(block, block, other, send, send).wait_send()

    def correlate():
        rows = own + 16
        for a in range(4):
            r4[:, 512 * a:512 * a + 512] = r[8 * a:8 * a + rows, :]
        acc = None
        for a in range(4):
            d = lax.dot_general(r4[:, 512 * a:512 * a + 512], w_ref[512 * a:512 * a + 512, :], NT,
                                preferred_element_type=F32)
            acc = d if acc is None else acc + d
        q[...] = acc
        s = q[0:own + 8, 0:LANES]
        for b in range(1, 4):
            s = s + q[2 * b:2 * b + own + 8, LANES * b:LANES * b + LANES]
        return s[0:own, 0:FACTORS] + s[1:own + 1, FACTORS:2 * FACTORS]

    def stack():
        for j in range(LAGS // 2):
            hst[:, LANES * j:LANES * j + LANES] = (
                df[HALO - 2 * j:HALO - 2 * j + own + HALO, :].astype(BF16))

    def convolve():
        rows = own + HALO
        r[0:rows, :] = jnp.dot(hst[...], w_ref[...], preferred_element_type=F32).astype(BF16)
        tail = r[own:rows, :]
        r[own:rows, :] = jnp.where(last, jnp.zeros_like(tail), tail)

    def put_field(field):
        df[HALO:HALO + own, 0:FACTORS] = field
        df[HALO + 1:HALO + own + 1, FACTORS:2 * FACTORS] = field

    def put_gram(field):
        hi = field.astype(BF16)
        lo = (field - hi.astype(F32)).astype(BF16)
        fa[:, 0:FACTORS] = hi
        fa[:, FACTORS:2 * FACTORS] = lo

    def put_halos(it):
        from_left = halo_l[it]
        from_left = jnp.where(first, jnp.zeros_like(from_left), from_left)
        from_right = halo_r[it]
        df[0:HALO, 0:FACTORS] = from_left
        df[1:HALO + 1, FACTORS:2 * FACTORS] = from_left
        df[HALO + own:own + 2 * HALO, 0:FACTORS] = from_right
        df[HALO + own + 1:own + 2 * HALO, FACTORS:2 * FACTORS] = from_right[0:HALO - 1]

    def send_halos(it, field):
        halo_src[it, 0] = field[0:HALO]
        halo_src[it, 1] = field[own - HALO:own]
        slots = (slot(), slot(), slot())
        remote(halo_src.at[it, 0], halo_r.at[it], left, slots[0], slots[1])
        remote(halo_src.at[it, 1], halo_l.at[it], right, slots[0], slots[2])
        return slots

    def halos_here(it, slots):
        arrival(halo_r.at[it], slots[1])
        arrival(halo_l.at[it], slots[2])

    row_id = lax.broadcasted_iota(jnp.int32, (FACTORS, FACTORS), 0)
    col_id = lax.broadcasted_iota(jnp.int32, (FACTORS, FACTORS), 1)
    off_mask = jnp.where(row_id == col_id, 0.0, penalty_weight / total).astype(F32)

    got[core, y, x, z] = src[...]
    pairs = nz // 2
    pair = z // 2
    base = [slot() for _ in range(pairs)]
    piece = got.at[core, y, x, z]
    piece_send = slot()
    remote(src, piece, at(pair * 2 + 1 - z % 2, x, core, y), piece_send, base[0])
    for p in [1, pairs - 1] + list(range(2, pairs - 1)):
        for b in range(2):
            there = (pair + pairs - p) % pairs * 2 + b
            remote(src, piece, at(there, x, core, y), piece_send, base[p])
    data_send, data_recv = slot(), slot()
    for d in range(1, ny):
        there = (y + d) % ny
        columns = pl.ds(pl.multiple_of(there * own, own), own)
        remote(x_ref.at[:, columns], tiles.at[y], along_y[d - 1], data_send, data_recv)

    def gram_start(it):
        gg = lax.dot_general(fa[...], fa[...], TN, preferred_element_type=F32)
        gram = (gg[0:FACTORS, 0:FACTORS] + gg[0:FACTORS, FACTORS:] + gg[FACTORS:, 0:FACTORS]
                + gg[FACTORS:, FACTORS:])
        packed = jnp.concatenate([gram[0:32], gram[32:64]], axis=1)
        gsrc[it, 0] = packed[0:16]
        gsrc[it, 1] = packed[16:32]
        slots = [slot() for _ in range(8)]
        remote(gsrc.at[it, 1 - core], cbuf.at[it], other, slots[0], slots[1])
        return slots

    def gram_across(it, slots):
        arrival(cbuf.at[it], slots[1])
        spot = x * ny + y
        xybuf[it, spot] = gsrc[it, core] + cbuf[it]
        for dev in across:
            remote(xybuf.at[it, spot], xybuf.at[it, spot], dev, slots[2], slots[3])

    def gram_along(it, slots):
        arrival(xybuf.at[it, pl.ds(0, NX * ny - 1)], slots[3])
        zbuf[it, z] = sum(xybuf[it, i] for i in range(NX * ny))
        for dev in along_z:
            remote(zbuf.at[it, z], zbuf.at[it, z], dev, slots[4], slots[5])

    def gram_back(it, slots):
        arrival(zbuf.at[it, pl.ds(0, nz - 1)], slots[5])
        part[it] = sum(zbuf[it, i] for i in range(nz))
        remote(part.at[it], gtot.at[it], other, slots[6], slots[7])

    def gram_sent(it, slots):
        departure(gsrc.at[it, 0], slots[0])
        departure(xybuf.at[it, pl.ds(0, NX * ny - 1)], slots[2])
        departure(zbuf.at[it, pl.ds(0, nz - 1)], slots[4])
        departure(part.at[it], slots[6])

    def gram_end(it, slots):
        arrival(gtot.at[it], slots[7])
        ours, theirs = part[it], gtot[it]
        low = jnp.where(core == 0, ours, theirs)
        high = jnp.where(core == 0, theirs, ours)
        packed = jnp.concatenate([low, high], axis=0)
        return jnp.concatenate([packed[:, 0:FACTORS], packed[:, FACTORS:]], axis=0) * off_mask

    def update(off, denom):
        off_hi = off.astype(BF16)
        off_lo = (off - off_hi.astype(F32)).astype(BF16)
        penalty = (jnp.dot(fa[...], jnp.concatenate([off_hi, off_hi], axis=0), preferred_element_type=F32)
                   + jnp.dot(fa[:, 0:FACTORS], off_lo, preferred_element_type=F32))
        return df[HALO:HALO + own, 0:FACTORS] * num[...] / (denom + penalty)

    partner_send = slot()

    def to_partner(yy, xx):
        here = slot()
        block = got.at[core, yy, xx]
        remote(block, block, other, partner_send, here)
        return yy, xx, here

    def from_partner(yy, xx, here):
        arrival(got.at[1 - core, yy, xx], here)
        spread(1 - core, yy, xx)

    def spread(cc, yy, xx):
        def one(i, _):
            k = (i * NX + xx) * NC + cc
            wf[yy, pl.ds(k, LAGS, stride=FACTORS), :] = got[cc, yy, xx, i].astype(F32)
            return 0

        lax.fori_loop(0, nz, one, 0, unroll=True)

    h_in.wait()
    field = h_own[...].T
    put_gram(field)
    gram_slots = gram_start(0)
    halo_slots = send_halos(0, field)

    order = [0, 1, pairs - 1] + list(range(2, pairs - 1))
    low_half, high_half = pl.ds(0, 16), pl.ds(16, 16)
    near_first = (1, 3, 2)

    def zs(p):
        return pl.ds((pair + p) % pairs * 2, 2)

    line_send = slot()
    from_x = [slot() for _ in range(pairs)]
    from_y = [slot() for _ in range(pairs)]
    for p in order:
        if p == 0:
            arrival(got.at[core, y, x, pair * 2 + 1 - z % 2], base[0])
        else:
            arrival(got.at[core, y, x, zs(p)], base[p])
        block = got.at[core, y, x, zs(p)]
        for d in near_first:
            remote(block, block, along_y[d - 1], line_send, from_y[p])
        for d in near_first:
            remote(block, block, along_x[d - 1], line_send, from_x[p])
        if p == 0:
            gram_across(0, gram_slots)
    early = [to_partner(y, x)]
    put_field(field)

    r[...] = jnp.zeros_like(r)
    x_in.wait()
    arrival(tiles.at[pl.ds(0, ny - 1)], data_recv)
    for c in range(ny):
        r[0:own, LANES * c:LANES * c + blocks] = tiles[c].astype(F32).T.astype(BF16)
    rim_src[...] = r[0:HALO, :]
    rim_send, rim_recv = slot(), slot()
    remote(rim_src, rim, left, rim_send, rim_recv)

    later_send = slot()
    later = {(d, e): slot() for d in range(1, ny) for e in range(1, NX)}
    for p in order:
        whole = p in order[:2]
        arrival(got.at[core, pl.ds(0, ny - 1), 0, pl.ds(0, 2)], from_y[p])
        for d in near_first:
            part_of = got.at[core, (y + ny - d) % ny, x, zs(p)]
            if not whole:
                part_of = got.at[core, (y + ny - d) % ny, x, zs(p), low_half]
            for e in near_first:
                remote(part_of, part_of, along_x[e - 1], later_send, later[d, e])
        arrival(got.at[core, 0, pl.ds(0, NX - 1), pl.ds(0, 2)], from_x[p])
        if not whole:
            for d in near_first:
                part_of = got.at[core, y, (x + NX - d) % NX, zs(p), high_half]
                for e in near_first:
                    remote(part_of, part_of, along_y[e - 1], later_send, later[e, d])
        if p == order[0]:
            gram_along(0, gram_slots)
    for d in range(1, NX):
        yy, xx = (y + ny - d) % ny, (x + NX - d) % NX
        early += [to_partner(yy, x), to_partner(y, xx)]
    gram_back(0, gram_slots)
    halos_here(0, halo_slots)
    put_halos(0)
    stack()
    arrival(rim, rim_recv)
    tail = rim[...]
    r[own:own + HALO, :] = jnp.where(last, jnp.zeros_like(tail), tail)
    for yy, xx, _ in early:
        spread(core, yy, xx)
    for entry in early:
        from_partner(*entry)
    late = []
    for (d, e), here in later.items():
        yy, xx = (y + ny - d) % ny, (x + NX - e) % NX
        arrival(got.at[core, yy, xx], here)
        late.append(to_partner(yy, xx))
        spread(core, yy, xx)
    off = gram_end(0, gram_slots)
    for entry in late:
        from_partner(*entry)

    def narrow(i, _):
        rows = pl.ds(pl.multiple_of(i * LANES, LANES), LANES)
        for yy in range(ny):
            w_ref[rows, LANES * yy:LANES * yy + LANES] = wf[yy, rows, :].astype(BF16)
        return 0

    lax.fori_loop(0, LAGS * FACTORS // LANES, narrow, 0)
    num[...] = correlate()
    convolve()
    denom = correlate()
    field = update(off, denom)

    def to_all_blocks(value, everyone_has):
        everyone_has[y] = value.T
        slots = (slot(), slot())
        for dev in along_y:
            remote(everyone_has.at[y], everyone_has.at[y], dev, *slots)
        return slots

    for it in range(1, ITERS):
        put_gram(field)
        before = gram_slots, halo_slots
        gram_slots = gram_start(it)
        halo_slots = send_halos(it, field)
        put_field(field)
        gram_across(it, gram_slots)
        if it == ITERS - 1:
            f_slots = to_all_blocks(field, all_f)
        gram_sent(it - 1, before[0])
        departure(halo_src.at[it - 1], before[1][0])
        if it == 1:
            departure(got.at[0, 0, 0, pl.ds(0, nz - 1)], piece_send)
            departure(tiles.at[pl.ds(0, ny - 1)], data_send)
            departure(rim_src, rim_send)
            departure(got.at[0, pl.ds(0, 3), pl.ds(0, 2)], line_send)
            departure(got.at[0, pl.ds(0, 3), pl.ds(0, 3)], later_send)
            departure(got.at[0], partner_send)
        halos_here(it, halo_slots)
        put_halos(it)
        stack()
        convolve()
        denom = correlate()
        gram_along(it, gram_slots)
        if it == ITERS - 1:
            d_slots = to_all_blocks(denom, all_d)
            departure(all_n.at[pl.ds(0, ny - 1)], n_slots[0])
            arrival(all_n.at[pl.ds(0, ny - 1)], n_slots[1])
            arrival(all_f.at[pl.ds(0, ny - 1)], f_slots[1])
            for yy in range(ny):
                f = all_f[yy]
                hi = f.astype(BF16)
                fb[yy, 0:FACTORS, :] = hi
                fb[yy, FACTORS:2 * FACTORS, :] = (f - hi.astype(F32)).astype(BF16)
                all_a[yy] = f * all_n[yy]
        elif it == 1:
            n_slots = to_all_blocks(num[...], all_n)
        gram_back(it, gram_slots)
        off = gram_end(it, gram_slots)
        if it < ITERS - 1:
            field = update(off, denom)

    off_hi = off.astype(BF16)
    off_lo = (off - off_hi.astype(F32)).astype(BF16)
    twice = jnp.concatenate([off_hi, off_hi], axis=1)
    departure(all_f.at[pl.ds(0, ny - 1)], f_slots[0])
    arrival(all_d.at[pl.ds(0, ny - 1)], d_slots[1])
    for yy in range(ny):
        penalty = (jnp.dot(twice, fb[yy], preferred_element_type=F32)
                   + jnp.dot(off_lo, fb[yy, 0:FACTORS, :], preferred_element_type=F32))
        out_ref[:, own * yy:own * yy + own] = all_a[yy] / (all_d[yy] + penalty)
    departure(all_d.at[pl.ds(0, ny - 1)], d_slots[0])
    assert count[0] == SLOTS, count[0]
    departure(halo_src.at[ITERS - 1], halo_slots[0])
    gram_sent(ITERS - 1, gram_slots)


def on_device(data, motifs, loadings):
    ntm, ny = lax.axis_size("tm"), lax.axis_size("chan")
    blocks, steps = data.shape
    own = steps // ny
    nz = ntm // (NX * NC)
    V = pl.BlockSpec(memory_space=pltpu.VMEM)
    A = pl.BlockSpec(memory_space=pl.ANY)
    vm = pltpu.VMEM
    return pl.pallas_call(
        functools.partial(kernel, nz, ny, float(steps * ntm)),
        out_shape=jax.ShapeDtypeStruct((FACTORS, steps), F32),
        in_specs=[V, A, A],
        out_specs=V,
        scratch_shapes=[
            vm((LAGS, LANES), BF16),
            vm((NC, ny, NX, nz, LAGS, LANES), BF16),
            vm((ny, LAGS * FACTORS, LANES), F32),
            vm((LAGS * FACTORS, ny * LANES), BF16),
            vm((ny, blocks, own), BF16),
            vm((FACTORS, own), F32),
            vm((HALO, ny * LANES), BF16),
            vm((HALO, ny * LANES), BF16),
            vm((own + 2 * HALO, 2 * FACTORS), F32),
            vm((own + HALO, LAGS * FACTORS), BF16),
            vm((own + HALO + 16, ny * LANES), BF16),
            vm((own + 16, 4 * ny * LANES), BF16),
            vm((own + 16, 4 * LANES), F32),
            vm((own, FACTORS), F32),
            vm((own, 2 * FACTORS), BF16),
            vm((ITERS, 2, HALO, FACTORS), F32),
            vm((ITERS, HALO, FACTORS), F32),
            vm((ITERS, HALO, FACTORS), F32),
            vm((ITERS, 2, 16, LANES), F32),
            vm((ITERS, 16, LANES), F32),
            vm((ITERS, 16, LANES), F32),
            vm((ITERS, NX * ny, 16, LANES), F32),
            vm((ITERS, nz, 16, LANES), F32),
            vm((ITERS, 16, LANES), F32),
            vm((ny, FACTORS, own), F32),
            vm((ny, FACTORS, own), F32),
            vm((ny, FACTORS, own), F32),
            vm((ny, FACTORS, own), F32),
            vm((ny, 2 * FACTORS, own), BF16),
            pltpu.SemaphoreType.DMA((SLOTS,)),
            pltpu.SemaphoreType.DMA((2,)),
        ],
        compiler_params=pltpu.CompilerParams(collective_id=0, has_side_effects=True),
    )(motifs.T, data, loadings)


def solution(mesh):
    in_specs = (P("chan", "tm"), P("chan", "tm"), P(None, "tm"))
    out_specs = P(None, "tm")
    return jax.shard_map(
        on_device, mesh=mesh, in_specs=in_specs, out_specs=out_specs, check_vma=False
    )
```

```python
import functools

import jax
import jax.numpy as jnp
from jax import lax
from jax.experimental import pallas as pl
from jax.experimental.pallas import tpu as pltpu
from jax.sharding import PartitionSpec as P

FACTORS = 64
LAGS = 32
ITERS = 3
LANES = 128
HALO = LAGS
SLOTS = 86
penalty_weight = 0.2

F32 = jnp.float32
BF16 = jnp.bfloat16
MESH = pl.DeviceIdType.MESH
NT = (((1,), (1,)), ((), ()))
TN = (((0,), (0,)), ((), ()))

NX = 4
NC = 2


def kernel(nz, ny, total, m_ref, x_ref, h_ref, out_ref, src, got, wf, w_ref, tiles, h_own, rim_src, rim,
           df, hst, r, r4, q, num, fa, halo_src, halo_l, halo_r, gsrc, cbuf, part, xybuf, zbuf, gtot,
           all_n, all_f, all_d, all_e, all_a, result, fb, sem, in_sem):
    blocks = m_ref.shape[1]
    own = h_ref.shape[1] // ny
    tm = lax.axis_index("tm")
    y = lax.axis_index("chan")
    core = tm % NC
    x = (tm // NC) % NX
    z = tm // (NC * NX)
    ntm = nz * NX * NC

    def at(zz, xx, cc, yy):
        return ((zz * NX + xx) * NC + cc, yy)

    spot = tm * ny + y
    right_spot = (spot + 1) % (ntm * ny)
    left_spot = (spot + ntm * ny - 1) % (ntm * ny)
    right = (right_spot // ny, right_spot % ny)
    left = (left_spot // ny, left_spot % ny)
    first = spot == 0
    last = spot == ntm * ny - 1

    other = at(z, x, 1 - core, y)
    along_x = [at(z, (x + d) % NX, core, y) for d in range(1, NX)]
    along_y = [at(z, x, core, (y + d) % ny) for d in range(1, ny)]
    across = [at(z, (x + d) % NX, core, (y + e) % ny) for d in range(NX) for e in range(ny) if d or e]
    along_z = [at((z + d) % nz, x, core, y) for d in range(1, nz)]

    mine = pl.ds(pl.multiple_of(y * own, own), own)
    h_in = pltpu.make_async_copy(h_ref.at[:, mine], h_own, in_sem.at[0])
    h_in.start()
    x_in = pltpu.make_async_copy(x_ref.at[:, mine], tiles.at[y], in_sem.at[1])
    x_in.start()

    barrier = pltpu.get_barrier_semaphore()
    everyone = [other, left, right] + across + along_z
    for device in everyone:
        pl.semaphore_signal(barrier, inc=1, device_id=device, device_id_type=MESH)
    src[...] = jnp.zeros_like(src)
    src[:, 0:blocks] = m_ref[...]
    df[0:8, :] = jnp.zeros((8, 2 * FACTORS), F32)
    pl.semaphore_wait(barrier, len(everyone))

    count = [0]

    def slot():
        count[0] += 1
        return count[0] - 1

    def copy_of(src, dst, device, send, recv):
        return pltpu.make_async_remote_copy(
            src_ref=src, dst_ref=dst, send_sem=sem.at[send], recv_sem=sem.at[recv],
            device_id=device, device_id_type=MESH)

    def remote(src, dst, device, send, recv):
        copy_of(src, dst, device, send, recv).start()

    def arrival(block, recv):
        copy_of(block, block, other, recv, recv).wait_recv()

    def departure(block, send):
        copy_of(block, block, other, send, send).wait_send()

    def correlate():
        rows = own + 16
        for a in range(4):
            r4[:, 512 * a:512 * a + 512] = r[8 * a:8 * a + rows, :]
        acc = None
        for a in range(4):
            d = lax.dot_general(r4[:, 512 * a:512 * a + 512], w_ref[512 * a:512 * a + 512, :], NT,
                                preferred_element_type=F32)
            acc = d if acc is None else acc + d
        q[...] = acc
        s = q[0:own + 8, 0:LANES]
        for b in range(1, 4):
            s = s + q[2 * b:2 * b + own + 8, LANES * b:LANES * b + LANES]
        return s[0:own, 0:FACTORS] + s[1:own + 1, FACTORS:2 * FACTORS]

    def stack():
        for j in range(LAGS // 2):
            hst[:, LANES * j:LANES * j + LANES] = (
                df[HALO - 2 * j:HALO - 2 * j + own + HALO, :].astype(BF16))

    def convolve():
        rows = own + HALO
        r[0:rows, :] = jnp.dot(hst[...], w_ref[...], preferred_element_type=F32).astype(BF16)
        tail = r[own:rows, :]
        r[own:rows, :] = jnp.where(last, jnp.zeros_like(tail), tail)

    def put_field(field):
        df[HALO:HALO + own, 0:FACTORS] = field
        df[HALO + 1:HALO + own + 1, FACTORS:2 * FACTORS] = field

    def put_gram(field):
        hi = field.astype(BF16)
        lo = (field - hi.astype(F32)).astype(BF16)
        fa[:, 0:FACTORS] = hi
        fa[:, FACTORS:2 * FACTORS] = lo

    def put_halos(it):
        from_left = halo_l[it]
        from_left = jnp.where(first, jnp.zeros_like(from_left), from_left)
        from_right = halo_r[it]
        df[0:HALO, 0:FACTORS] = from_left
        df[1:HALO + 1, FACTORS:2 * FACTORS] = from_left
        df[HALO + own:own + 2 * HALO, 0:FACTORS] = from_right
        df[HALO + own + 1:own + 2 * HALO, FACTORS:2 * FACTORS] = from_right[0:HALO - 1]

    def send_halos(it, field):
        halo_src[it, 0] = field[0:HALO]
        halo_src[it, 1] = field[own - HALO:own]
        slots = (slot(), slot(), slot())
        remote(halo_src.at[it, 0], halo_r.at[it], left, slots[0], slots[1])
        remote(halo_src.at[it, 1], halo_l.at[it], right, slots[0], slots[2])
        return slots

    def halos_here(it, slots):
        arrival(halo_r.at[it], slots[1])
        arrival(halo_l.at[it], slots[2])

    row_id = lax.broadcasted_iota(jnp.int32, (FACTORS, FACTORS), 0)
    col_id = lax.broadcasted_iota(jnp.int32, (FACTORS, FACTORS), 1)
    off_mask = jnp.where(row_id == col_id, 0.0, penalty_weight / total).astype(F32)

    got[core, y, x, z] = src[...]
    pairs = nz // 2
    pair = z // 2
    base = [slot() for _ in range(pairs)]
    piece = got.at[core, y, x, z]
    piece_send = slot()
    remote(src, piece, at(pair * 2 + 1 - z % 2, x, core, y), piece_send, base[0])
    for p in [1, pairs - 1] + list(range(2, pairs - 1)):
        for b in range(2):
            there = (pair + pairs - p) % pairs * 2 + b
            remote(src, piece, at(there, x, core, y), piece_send, base[p])
    data_send, data_recv = slot(), slot()
    for d in range(1, ny):
        there = (y + d) % ny
        columns = pl.ds(pl.multiple_of(there * own, own), own)
        remote(x_ref.at[:, columns], tiles.at[y], along_y[d - 1], data_send, data_recv)

    def gram_start(it):
        gg = lax.dot_general(fa[...], fa[...], TN, preferred_element_type=F32)
        gram = (gg[0:FACTORS, 0:FACTORS] + gg[0:FACTORS, FACTORS:] + gg[FACTORS:, 0:FACTORS]
                + gg[FACTORS:, FACTORS:])
        packed = jnp.concatenate([gram[0:32], gram[32:64]], axis=1)
        gsrc[it, 0] = packed[0:16]
        gsrc[it, 1] = packed[16:32]
        slots = [slot() for _ in range(8)]
        remote(gsrc.at[it, 1 - core], cbuf.at[it], other, slots[0], slots[1])
        return slots

    def gram_across(it, slots):
        arrival(cbuf.at[it], slots[1])
        spot = x * ny + y
        xybuf[it, spot] = gsrc[it, core] + cbuf[it]
        for dev in across:
            remote(xybuf.at[it, spot], xybuf.at[it, spot], dev, slots[2], slots[3])

    def gram_along(it, slots):
        arrival(xybuf.at[it, pl.ds(0, NX * ny - 1)], slots[3])
        zbuf[it, z] = sum(xybuf[it, i] for i in range(NX * ny))
        for dev in along_z:
            remote(zbuf.at[it, z], zbuf.at[it, z], dev, slots[4], slots[5])

    def gram_back(it, slots):
        arrival(zbuf.at[it, pl.ds(0, nz - 1)], slots[5])
        part[it] = sum(zbuf[it, i] for i in range(nz))
        remote(part.at[it], gtot.at[it], other, slots[6], slots[7])

    def gram_sent(it, slots):
        departure(gsrc.at[it, 0], slots[0])
        departure(xybuf.at[it, pl.ds(0, NX * ny - 1)], slots[2])
        departure(zbuf.at[it, pl.ds(0, nz - 1)], slots[4])
        departure(part.at[it], slots[6])

    def gram_end(it, slots):
        arrival(gtot.at[it], slots[7])
        ours, theirs = part[it], gtot[it]
        low = jnp.where(core == 0, ours, theirs)
        high = jnp.where(core == 0, theirs, ours)
        packed = jnp.concatenate([low, high], axis=0)
        return jnp.concatenate([packed[:, 0:FACTORS], packed[:, FACTORS:]], axis=0) * off_mask

    def update(off, denom):
        off_hi = off.astype(BF16)
        off_lo = (off - off_hi.astype(F32)).astype(BF16)
        penalty = (jnp.dot(fa[...], jnp.concatenate([off_hi, off_hi], axis=0), preferred_element_type=F32)
                   + jnp.dot(fa[:, 0:FACTORS], off_lo, preferred_element_type=F32))
        return df[HALO:HALO + own, 0:FACTORS] * num[...] / (denom + penalty)

    partner_send = slot()

    def to_partner(yy, xx):
        here = slot()
        block = got.at[core, yy, xx]
        remote(block, block, other, partner_send, here)
        return yy, xx, here

    def from_partner(yy, xx, here):
        arrival(got.at[1 - core, yy, xx], here)
        spread(1 - core, yy, xx)

    def spread(cc, yy, xx):
        def one(i, _):
            k = (i * NX + xx) * NC + cc
            wf[yy, pl.ds(k, LAGS, stride=FACTORS), :] = got[cc, yy, xx, i].astype(F32)
            return 0

        lax.fori_loop(0, nz, one, 0, unroll=True)

    h_in.wait()
    field = h_own[...].T
    put_gram(field)
    gram_slots = gram_start(0)
    halo_slots = send_halos(0, field)

    order = [0, 1, pairs - 1] + list(range(2, pairs - 1))
    low_half, high_half = pl.ds(0, 16), pl.ds(16, 16)
    near_first = (1, 3, 2)

    def zs(p):
        return pl.ds((pair + p) % pairs * 2, 2)

    line_send = slot()
    from_x = [slot() for _ in range(pairs)]
    from_y = [slot() for _ in range(pairs)]
    for p in order:
        if p == 0:
            arrival(got.at[core, y, x, pair * 2 + 1 - z % 2], base[0])
        else:
            arrival(got.at[core, y, x, zs(p)], base[p])
        block = got.at[core, y, x, zs(p)]
        for d in near_first:
            remote(block, block, along_y[d - 1], line_send, from_y[p])
        for d in near_first:
            remote(block, block, along_x[d - 1], line_send, from_x[p])
        if p == 0:
            gram_across(0, gram_slots)
    early = [to_partner(y, x)]
    put_field(field)

    r[...] = jnp.zeros_like(r)
    x_in.wait()
    arrival(tiles.at[pl.ds(0, ny - 1)], data_recv)
    for c in range(ny):
        r[0:own, LANES * c:LANES * c + blocks] = tiles[c].astype(F32).T.astype(BF16)
    rim_src[...] = r[0:HALO, :]
    rim_send, rim_recv = slot(), slot()
    remote(rim_src, rim, left, rim_send, rim_recv)

    later_send = slot()
    later = {(d, e): slot() for d in range(1, ny) for e in range(1, NX)}
    for p in order:
        whole = p in order[:2]
        arrival(got.at[core, pl.ds(0, ny - 1), 0, pl.ds(0, 2)], from_y[p])
        for d in near_first:
            part_of = got.at[core, (y + ny - d) % ny, x, zs(p)]
            if not whole:
                part_of = got.at[core, (y + ny - d) % ny, x, zs(p), low_half]
            for e in near_first:
                remote(part_of, part_of, along_x[e - 1], later_send, later[d, e])
        arrival(got.at[core, 0, pl.ds(0, NX - 1), pl.ds(0, 2)], from_x[p])
        if not whole:
            for d in near_first:
                part_of = got.at[core, y, (x + NX - d) % NX, zs(p), high_half]
                for e in near_first:
                    remote(part_of, part_of, along_y[e - 1], later_send, later[e, d])
        if p == order[0]:
            gram_along(0, gram_slots)
    for d in range(1, NX):
        yy, xx = (y + ny - d) % ny, (x + NX - d) % NX
        early += [to_partner(yy, x), to_partner(y, xx)]
    gram_back(0, gram_slots)
    halos_here(0, halo_slots)
    put_halos(0)
    stack()
    arrival(rim, rim_recv)
    tail = rim[...]
    r[own:own + HALO, :] = jnp.where(last, jnp.zeros_like(tail), tail)
    for yy, xx, _ in early:
        spread(core, yy, xx)
    for entry in early:
        from_partner(*entry)
    late = []
    for (d, e), here in later.items():
        yy, xx = (y + ny - d) % ny, (x + NX - e) % NX
        arrival(got.at[core, yy, xx], here)
        late.append(to_partner(yy, xx))
        spread(core, yy, xx)
    off = gram_end(0, gram_slots)
    for entry in late:
        from_partner(*entry)

    def narrow(i, _):
        rows = pl.ds(pl.multiple_of(i * LANES, LANES), LANES)
        for yy in range(ny):
            w_ref[rows, LANES * yy:LANES * yy + LANES] = wf[yy, rows, :].astype(BF16)
        return 0

    lax.fori_loop(0, LAGS * FACTORS // LANES, narrow, 0)
    def to_all_blocks(value, everyone_has):
        everyone_has[y] = value.T
        slots = (slot(), slot())
        for dev in along_y:
            remote(everyone_has.at[y], everyone_has.at[y], dev, *slots)
        return slots

    def all_here(everyone_has, slots):
        departure(everyone_has.at[pl.ds(0, ny - 1)], slots[0])
        arrival(everyone_has.at[pl.ds(0, ny - 1)], slots[1])

    def put_block(yy, f):
        hi = f.astype(BF16)
        fb[yy, 0:FACTORS, :] = hi
        fb[yy, FACTORS:2 * FACTORS, :] = (f - hi.astype(F32)).astype(BF16)
        all_a[yy] = f * all_n[yy]

    def updated_block(yy, off, denom):
        off_hi = off.astype(BF16)
        off_lo = (off - off_hi.astype(F32)).astype(BF16)
        penalty = (jnp.dot(jnp.concatenate([off_hi, off_hi], axis=1), fb[yy], preferred_element_type=F32)
                   + jnp.dot(off_lo, fb[yy, 0:FACTORS, :], preferred_element_type=F32))
        return all_a[yy] / (denom + penalty)

    num[...] = correlate()
    n_slots = to_all_blocks(num[...], all_n)
    convolve()
    denom = correlate()
    field = update(off, denom)

    for it in range(1, ITERS):
        put_gram(field)
        before = gram_slots, halo_slots
        gram_slots = gram_start(it)
        halo_slots = send_halos(it, field)
        put_field(field)
        gram_across(it, gram_slots)
        if it == ITERS - 2:
            f_slots = to_all_blocks(field, all_f)
        gram_sent(it - 1, before[0])
        departure(halo_src.at[it - 1], before[1][0])
        if it == 1:
            departure(got.at[0, 0, 0, pl.ds(0, nz - 1)], piece_send)
            departure(tiles.at[pl.ds(0, ny - 1)], data_send)
            departure(rim_src, rim_send)
            departure(got.at[0, pl.ds(0, 3), pl.ds(0, 2)], line_send)
            departure(got.at[0, pl.ds(0, 3), pl.ds(0, 3)], later_send)
            departure(got.at[0], partner_send)
        halos_here(it, halo_slots)
        put_halos(it)
        stack()
        convolve()
        denom = correlate()
        gram_along(it, gram_slots)
        if it == ITERS - 2:
            d_slots = to_all_blocks(denom, all_d)
        if it == ITERS - 1:
            end_slots = to_all_blocks(denom, all_e)
            all_here(all_n, n_slots)
            all_here(all_f, f_slots)
            all_here(all_d, d_slots)
            for yy in range(ny):
                put_block(yy, all_f[yy])
                put_block(yy, updated_block(yy, off, all_d[yy]))
        gram_back(it, gram_slots)
        off = gram_end(it, gram_slots)
        if it < ITERS - 1:
            field = update(off, denom)

    all_here(all_e, end_slots)
    outs = []
    for yy in range(ny):
        result[yy] = updated_block(yy, off, all_e[yy])
        outs.append(pltpu.make_async_copy(result.at[yy], out_ref.at[:, pl.ds(own * yy, own)], in_sem.at[2 + yy]))
        outs[-1].start()
    departure(halo_src.at[ITERS - 1], halo_slots[0])
    gram_sent(ITERS - 1, gram_slots)
    for c in outs:
        c.wait()
    assert count[0] == SLOTS, count[0]


def on_device(data, motifs, loadings):
    ntm, ny = lax.axis_size("tm"), lax.axis_size("chan")
    blocks, steps = data.shape
    own = steps // ny
    nz = ntm // (NX * NC)
    V = pl.BlockSpec(memory_space=pltpu.VMEM)
    A = pl.BlockSpec(memory_space=pl.ANY)
    vm = pltpu.VMEM
    return pl.pallas_call(
        functools.partial(kernel, nz, ny, float(steps * ntm)),
        out_shape=jax.ShapeDtypeStruct((FACTORS, steps), F32),
        in_specs=[V, A, A],
        out_specs=A,
        scratch_shapes=[
            vm((LAGS, LANES), BF16),
            vm((NC, ny, NX, nz, LAGS, LANES), BF16),
            vm((ny, LAGS * FACTORS, LANES), F32),
            vm((LAGS * FACTORS, ny * LANES), BF16),
            vm((ny, blocks, own), BF16),
            vm((FACTORS, own), F32),
            vm((HALO, ny * LANES), BF16),
            vm((HALO, ny * LANES), BF16),
            vm((own + 2 * HALO, 2 * FACTORS), F32),
            vm((own + HALO, LAGS * FACTORS), BF16),
            vm((own + HALO + 16, ny * LANES), BF16),
            vm((own + 16, 4 * ny * LANES), BF16),
            vm((own + 16, 4 * LANES), F32),
            vm((own, FACTORS), F32),
            vm((own, 2 * FACTORS), BF16),
            vm((ITERS, 2, HALO, FACTORS), F32),
            vm((ITERS, HALO, FACTORS), F32),
            vm((ITERS, HALO, FACTORS), F32),
            vm((ITERS, 2, 16, LANES), F32),
            vm((ITERS, 16, LANES), F32),
            vm((ITERS, 16, LANES), F32),
            vm((ITERS, NX * ny, 16, LANES), F32),
            vm((ITERS, nz, 16, LANES), F32),
            vm((ITERS, 16, LANES), F32),
            vm((ny, FACTORS, own), F32),
            vm((ny, FACTORS, own), F32),
            vm((ny, FACTORS, own), F32),
            vm((ny, FACTORS, own), F32),
            vm((ny, FACTORS, own), F32),
            vm((ny, FACTORS, own), F32),
            vm((ny, 2 * FACTORS, own), BF16),
            pltpu.SemaphoreType.DMA((SLOTS,)),
            pltpu.SemaphoreType.DMA((2 + ny,)),
        ],
        compiler_params=pltpu.CompilerParams(collective_id=0, has_side_effects=True),
    )(motifs.T, data, loadings)


def solution(mesh):
    in_specs = (P("chan", "tm"), P("chan", "tm"), P(None, "tm"))
    out_specs = P(None, "tm")
    return jax.shard_map(
        on_device, mesh=mesh, in_specs=in_specs, out_specs=out_specs, check_vma=False
    )
```

```python
import functools

import jax
import jax.numpy as jnp
from jax import lax
from jax.experimental import pallas as pl
from jax.experimental.pallas import tpu as pltpu
from jax.sharding import PartitionSpec as P

FACTORS = 64
LAGS = 32
ITERS = 3
LANES = 128
HALO = LAGS
SLOTS = 84
penalty_weight = 0.2

F32 = jnp.float32
BF16 = jnp.bfloat16
MESH = pl.DeviceIdType.MESH
NT = (((1,), (1,)), ((), ()))
TN = (((0,), (0,)), ((), ()))

NX = 4
NC = 2


def kernel(nz, ny, total, m_ref, x_ref, h_ref, out_ref, src, got, wf, w_ref, tiles, h_own, rim_src, rim,
           df, hst, r, r4, q, num, fa, halo_src, halo_l, halo_r, gsrc, cbuf, part, xybuf, zbuf, gtot,
           all_n, all_f, all_d, all_a, fb, sem, in_sem):
    blocks = m_ref.shape[1]
    own = h_ref.shape[1] // ny
    tm = lax.axis_index("tm")
    y = lax.axis_index("chan")
    core = tm % NC
    x = (tm // NC) % NX
    z = tm // (NC * NX)
    ntm = nz * NX * NC

    def at(zz, xx, cc, yy):
        return ((zz * NX + xx) * NC + cc, yy)

    spot = tm * ny + y
    right_spot = (spot + 1) % (ntm * ny)
    left_spot = (spot + ntm * ny - 1) % (ntm * ny)
    right = (right_spot // ny, right_spot % ny)
    left = (left_spot // ny, left_spot % ny)
    first = spot == 0
    last = spot == ntm * ny - 1

    other = at(z, x, 1 - core, y)
    along_x = [at(z, (x + d) % NX, core, y) for d in range(1, NX)]
    along_y = [at(z, x, core, (y + d) % ny) for d in range(1, ny)]
    across = [at(z, (x + d) % NX, core, (y + e) % ny) for d in range(NX) for e in range(ny) if d or e]
    along_z = [at((z + d) % nz, x, core, y) for d in range(1, nz)]

    mine = pl.ds(pl.multiple_of(y * own, own), own)
    h_in = pltpu.make_async_copy(h_ref.at[:, mine], h_own, in_sem.at[0])
    h_in.start()
    x_in = pltpu.make_async_copy(x_ref.at[:, mine], tiles.at[y], in_sem.at[1])
    x_in.start()

    barrier = pltpu.get_barrier_semaphore()
    everyone = [other, left, right] + across + along_z
    for device in everyone:
        pl.semaphore_signal(barrier, inc=1, device_id=device, device_id_type=MESH)
    src[...] = jnp.zeros_like(src)
    src[:, 0:blocks] = m_ref[...]
    df[0:8, :] = jnp.zeros((8, 2 * FACTORS), F32)
    pl.semaphore_wait(barrier, len(everyone))

    count = [0]

    def slot():
        count[0] += 1
        return count[0] - 1

    def copy_of(src, dst, device, send, recv):
        return pltpu.make_async_remote_copy(
            src_ref=src, dst_ref=dst, send_sem=sem.at[send], recv_sem=sem.at[recv],
            device_id=device, device_id_type=MESH)

    def remote(src, dst, device, send, recv):
        copy_of(src, dst, device, send, recv).start()

    def arrival(block, recv):
        copy_of(block, block, other, recv, recv).wait_recv()

    def departure(block, send):
        copy_of(block, block, other, send, send).wait_send()

    def correlate():
        rows = own + 16
        for a in range(4):
            r4[:, 512 * a:512 * a + 512] = r[8 * a:8 * a + rows, :]
        acc = None
        for a in range(4):
            d = lax.dot_general(r4[:, 512 * a:512 * a + 512], w_ref[512 * a:512 * a + 512, :], NT,
                                preferred_element_type=F32)
            acc = d if acc is None else acc + d
        q[...] = acc
        s = q[0:own + 8, 0:LANES]
        for b in range(1, 4):
            s = s + q[2 * b:2 * b + own + 8, LANES * b:LANES * b + LANES]
        return s[0:own, 0:FACTORS] + s[1:own + 1, FACTORS:2 * FACTORS]

    def stack():
        for j in range(LAGS // 2):
            hst[:, LANES * j:LANES * j + LANES] = (
                df[HALO - 2 * j:HALO - 2 * j + own + HALO, :].astype(BF16))

    def convolve():
        rows = own + HALO
        r[0:rows, :] = jnp.dot(hst[...], w_ref[...], preferred_element_type=F32).astype(BF16)
        tail = r[own:rows, :]
        r[own:rows, :] = jnp.where(last, jnp.zeros_like(tail), tail)

    def put_field(field):
        df[HALO:HALO + own, 0:FACTORS] = field
        df[HALO + 1:HALO + own + 1, FACTORS:2 * FACTORS] = field

    def put_gram(field):
        hi = field.astype(BF16)
        lo = (field - hi.astype(F32)).astype(BF16)
        fa[:, 0:FACTORS] = hi
        fa[:, FACTORS:2 * FACTORS] = lo

    def put_halos(it):
        from_left = halo_l[it]
        from_left = jnp.where(first, jnp.zeros_like(from_left), from_left)
        from_right = halo_r[it]
        df[0:HALO, 0:FACTORS] = from_left
        df[1:HALO + 1, FACTORS:2 * FACTORS] = from_left
        df[HALO + own:own + 2 * HALO, 0:FACTORS] = from_right
        df[HALO + own + 1:own + 2 * HALO, FACTORS:2 * FACTORS] = from_right[0:HALO - 1]

    def send_halos(it, field):
        halo_src[it, 0] = field[0:HALO]
        halo_src[it, 1] = field[own - HALO:own]
        slots = (slot(), slot(), slot())
        remote(halo_src.at[it, 0], halo_r.at[it], left, slots[0], slots[1])
        remote(halo_src.at[it, 1], halo_l.at[it], right, slots[0], slots[2])
        return slots

    def halos_here(it, slots):
        arrival(halo_r.at[it], slots[1])
        arrival(halo_l.at[it], slots[2])

    row_id = lax.broadcasted_iota(jnp.int32, (FACTORS, FACTORS), 0)
    col_id = lax.broadcasted_iota(jnp.int32, (FACTORS, FACTORS), 1)
    off_mask = jnp.where(row_id == col_id, 0.0, penalty_weight / total).astype(F32)

    got[core, y, x, z] = src[...]
    pairs = nz // 2
    pair = z // 2
    base = [slot() for _ in range(pairs)]
    piece = got.at[core, y, x, z]
    piece_send = slot()
    remote(src, piece, at(pair * 2 + 1 - z % 2, x, core, y), piece_send, base[0])
    for p in [1, pairs - 1] + list(range(2, pairs - 1)):
        for b in range(2):
            there = (pair + pairs - p) % pairs * 2 + b
            remote(src, piece, at(there, x, core, y), piece_send, base[p])
    data_send, data_recv = slot(), slot()
    for d in range(1, ny):
        there = (y + d) % ny
        columns = pl.ds(pl.multiple_of(there * own, own), own)
        remote(x_ref.at[:, columns], tiles.at[y], along_y[d - 1], data_send, data_recv)

    def gram_start(it):
        gg = lax.dot_general(fa[...], fa[...], TN, preferred_element_type=F32)
        gram = (gg[0:FACTORS, 0:FACTORS] + gg[0:FACTORS, FACTORS:] + gg[FACTORS:, 0:FACTORS]
                + gg[FACTORS:, FACTORS:])
        packed = jnp.concatenate([gram[0:32], gram[32:64]], axis=1)
        gsrc[it, 0] = packed[0:16]
        gsrc[it, 1] = packed[16:32]
        slots = [slot() for _ in range(8)]
        remote(gsrc.at[it, 1 - core], cbuf.at[it], other, slots[0], slots[1])
        return slots

    def gram_across(it, slots):
        arrival(cbuf.at[it], slots[1])
        spot = x * ny + y
        xybuf[it, spot] = gsrc[it, core] + cbuf[it]
        for dev in across:
            remote(xybuf.at[it, spot], xybuf.at[it, spot], dev, slots[2], slots[3])

    def gram_along(it, slots):
        arrival(xybuf.at[it, pl.ds(0, NX * ny - 1)], slots[3])
        zbuf[it, z] = sum(xybuf[it, i] for i in range(NX * ny))
        for dev in along_z:
            remote(zbuf.at[it, z], zbuf.at[it, z], dev, slots[4], slots[5])

    def gram_back(it, slots):
        arrival(zbuf.at[it, pl.ds(0, nz - 1)], slots[5])
        part[it] = sum(zbuf[it, i] for i in range(nz))
        remote(part.at[it], gtot.at[it], other, slots[6], slots[7])

    def gram_sent(it, slots):
        departure(gsrc.at[it, 0], slots[0])
        departure(xybuf.at[it, pl.ds(0, NX * ny - 1)], slots[2])
        departure(zbuf.at[it, pl.ds(0, nz - 1)], slots[4])
        departure(part.at[it], slots[6])

    def gram_end(it, slots):
        arrival(gtot.at[it], slots[7])
        ours, theirs = part[it], gtot[it]
        low = jnp.where(core == 0, ours, theirs)
        high = jnp.where(core == 0, theirs, ours)
        packed = jnp.concatenate([low, high], axis=0)
        return jnp.concatenate([packed[:, 0:FACTORS], packed[:, FACTORS:]], axis=0) * off_mask

    def update(off, denom):
        off_hi = off.astype(BF16)
        off_lo = (off - off_hi.astype(F32)).astype(BF16)
        penalty = (jnp.dot(fa[...], jnp.concatenate([off_hi, off_hi], axis=0), preferred_element_type=F32)
                   + jnp.dot(fa[:, 0:FACTORS], off_lo, preferred_element_type=F32))
        return df[HALO:HALO + own, 0:FACTORS] * num[...] / (denom + penalty)

    partner_send = slot()

    def to_partner(yy, xx):
        here = slot()
        block = got.at[core, yy, xx]
        remote(block, block, other, partner_send, here)
        return yy, xx, here

    def from_partner(yy, xx, here):
        arrival(got.at[1 - core, yy, xx], here)
        spread(1 - core, yy, xx)

    def spread(cc, yy, xx):
        def one(i, _):
            k = (i * NX + xx) * NC + cc
            wf[yy, pl.ds(k, LAGS, stride=FACTORS), :] = got[cc, yy, xx, i].astype(F32)
            return 0

        lax.fori_loop(0, nz, one, 0, unroll=True)

    h_in.wait()
    field = h_own[...].T
    put_gram(field)
    gram_slots = gram_start(0)
    halo_slots = send_halos(0, field)

    order = [0, 1, pairs - 1] + list(range(2, pairs - 1))
    low_half, high_half = pl.ds(0, 16), pl.ds(16, 16)
    near_first = (1, 3, 2)

    def zs(p):
        return pl.ds((pair + p) % pairs * 2, 2)

    line_send = slot()
    from_x = [slot() for _ in range(pairs)]
    from_y = [slot() for _ in range(pairs)]
    for p in order:
        if p == 0:
            arrival(got.at[core, y, x, pair * 2 + 1 - z % 2], base[0])
        else:
            arrival(got.at[core, y, x, zs(p)], base[p])
        block = got.at[core, y, x, zs(p)]
        for d in near_first:
            remote(block, block, along_y[d - 1], line_send, from_y[p])
        for d in near_first:
            remote(block, block, along_x[d - 1], line_send, from_x[p])
        if p == 0:
            gram_across(0, gram_slots)
    early = [to_partner(y, x)]
    put_field(field)

    r[...] = jnp.zeros_like(r)
    x_in.wait()
    arrival(tiles.at[pl.ds(0, ny - 1)], data_recv)
    for c in range(ny):
        r[0:own, LANES * c:LANES * c + blocks] = tiles[c].astype(F32).T.astype(BF16)
    rim_src[...] = r[0:HALO, :]
    rim_send, rim_recv = slot(), slot()
    remote(rim_src, rim, left, rim_send, rim_recv)

    later_send = slot()
    later = {(d, e): slot() for d in range(1, ny) for e in range(1, NX)}
    for p in order:
        whole = p in order[:2]
        arrival(got.at[core, pl.ds(0, ny - 1), 0, pl.ds(0, 2)], from_y[p])
        for d in near_first:
            part_of = got.at[core, (y + ny - d) % ny, x, zs(p)]
            if not whole:
                part_of = got.at[core, (y + ny - d) % ny, x, zs(p), low_half]
            for e in near_first:
                remote(part_of, part_of, along_x[e - 1], later_send, later[d, e])
        arrival(got.at[core, 0, pl.ds(0, NX - 1), pl.ds(0, 2)], from_x[p])
        if not whole:
            for d in near_first:
                part_of = got.at[core, y, (x + NX - d) % NX, zs(p), high_half]
                for e in near_first:
                    remote(part_of, part_of, along_y[e - 1], later_send, later[e, d])
        if p == order[0]:
            gram_along(0, gram_slots)
    for d in range(1, NX):
        yy, xx = (y + ny - d) % ny, (x + NX - d) % NX
        early += [to_partner(yy, x), to_partner(y, xx)]
    gram_back(0, gram_slots)
    halos_here(0, halo_slots)
    put_halos(0)
    stack()
    arrival(rim, rim_recv)
    tail = rim[...]
    r[own:own + HALO, :] = jnp.where(last, jnp.zeros_like(tail), tail)
    for yy, xx, _ in early:
        spread(core, yy, xx)
    for entry in early:
        from_partner(*entry)
    late = []
    for (d, e), here in later.items():
        yy, xx = (y + ny - d) % ny, (x + NX - e) % NX
        arrival(got.at[core, yy, xx], here)
        late.append(to_partner(yy, xx))
        spread(core, yy, xx)
    off = gram_end(0, gram_slots)
    for entry in late:
        from_partner(*entry)

    def narrow(i, _):
        rows = pl.ds(pl.multiple_of(i * LANES, LANES), LANES)
        for yy in range(ny):
            w_ref[rows, LANES * yy:LANES * yy + LANES] = wf[yy, rows, :].astype(BF16)
        return 0

    lax.fori_loop(0, LAGS * FACTORS // LANES, narrow, 0)
    num[...] = correlate()
    convolve()
    denom = correlate()
    field = update(off, denom)

    def to_all_blocks(value, everyone_has):
        everyone_has[y] = value.T
        slots = (slot(), slot())
        for dev in along_y:
            remote(everyone_has.at[y], everyone_has.at[y], dev, *slots)
        return slots

    for it in range(1, ITERS):
        before = gram_slots, halo_slots
        halo_slots = send_halos(it, field)
        put_gram(field)
        gram_slots = gram_start(it)
        put_field(field)
        gram_across(it, gram_slots)
        if it == ITERS - 1:
            f_slots = to_all_blocks(field, all_f)
        gram_sent(it - 1, before[0])
        departure(halo_src.at[it - 1], before[1][0])
        if it == 1:
            departure(got.at[0, 0, 0, pl.ds(0, nz - 1)], piece_send)
            departure(tiles.at[pl.ds(0, ny - 1)], data_send)
            departure(rim_src, rim_send)
            departure(got.at[0, pl.ds(0, 3), pl.ds(0, 2)], line_send)
            departure(got.at[0, pl.ds(0, 3), pl.ds(0, 3)], later_send)
            departure(got.at[0], partner_send)
        halos_here(it, halo_slots)
        put_halos(it)
        stack()
        convolve()
        denom = correlate()
        gram_along(it, gram_slots)
        if it == ITERS - 1:
            d_slots = to_all_blocks(denom, all_d)
            departure(all_n.at[pl.ds(0, ny - 1)], n_slots[0])
            arrival(all_n.at[pl.ds(0, ny - 1)], n_slots[1])
            arrival(all_f.at[pl.ds(0, ny - 1)], f_slots[1])
            for yy in range(ny):
                f = all_f[yy]
                hi = f.astype(BF16)
                fb[yy, 0:FACTORS, :] = hi
                fb[yy, FACTORS:2 * FACTORS, :] = (f - hi.astype(F32)).astype(BF16)
                all_a[yy] = f * all_n[yy]
        elif it == 1:
            n_slots = to_all_blocks(num[...], all_n)
        gram_back(it, gram_slots)
        off = gram_end(it, gram_slots)
        if it < ITERS - 1:
            field = update(off, denom)

    off_hi = off.astype(BF16)
    off_lo = (off - off_hi.astype(F32)).astype(BF16)
    twice = jnp.concatenate([off_hi, off_hi], axis=1)
    departure(all_f.at[pl.ds(0, ny - 1)], f_slots[0])
    arrival(all_d.at[pl.ds(0, ny - 1)], d_slots[1])
    for yy in range(ny):
        penalty = (jnp.dot(twice, fb[yy], preferred_element_type=F32)
                   + jnp.dot(off_lo, fb[yy, 0:FACTORS, :], preferred_element_type=F32))
        out_ref[:, own * yy:own * yy + own] = all_a[yy] / (all_d[yy] + penalty)
    departure(all_d.at[pl.ds(0, ny - 1)], d_slots[0])
    assert count[0] == SLOTS, count[0]
    departure(halo_src.at[ITERS - 1], halo_slots[0])
    gram_sent(ITERS - 1, gram_slots)


def on_device(data, motifs, loadings):
    ntm, ny = lax.axis_size("tm"), lax.axis_size("chan")
    blocks, steps = data.shape
    own = steps // ny
    nz = ntm // (NX * NC)
    V = pl.BlockSpec(memory_space=pltpu.VMEM)
    A = pl.BlockSpec(memory_space=pl.ANY)
    vm = pltpu.VMEM
    return pl.pallas_call(
        functools.partial(kernel, nz, ny, float(steps * ntm)),
        out_shape=jax.ShapeDtypeStruct((FACTORS, steps), F32),
        in_specs=[V, A, A],
        out_specs=V,
        scratch_shapes=[
            vm((LAGS, LANES), BF16),
            vm((NC, ny, NX, nz, LAGS, LANES), BF16),
            vm((ny, LAGS * FACTORS, LANES), F32),
            vm((LAGS * FACTORS, ny * LANES), BF16),
            vm((ny, blocks, own), BF16),
            vm((FACTORS, own), F32),
            vm((HALO, ny * LANES), BF16),
            vm((HALO, ny * LANES), BF16),
            vm((own + 2 * HALO, 2 * FACTORS), F32),
            vm((own + HALO, LAGS * FACTORS), BF16),
            vm((own + HALO + 16, ny * LANES), BF16),
            vm((own + 16, 4 * ny * LANES), BF16),
            vm((own + 16, 4 * LANES), F32),
            vm((own, FACTORS), F32),
            vm((own, 2 * FACTORS), BF16),
            vm((ITERS, 2, HALO, FACTORS), F32),
            vm((ITERS, HALO, FACTORS), F32),
            vm((ITERS, HALO, FACTORS), F32),
            vm((ITERS, 2, 16, LANES), F32),
            vm((ITERS, 16, LANES), F32),
            vm((ITERS, 16, LANES), F32),
            vm((ITERS, NX * ny, 16, LANES), F32),
            vm((ITERS, nz, 16, LANES), F32),
            vm((ITERS, 16, LANES), F32),
            vm((ny, FACTORS, own), F32),
            vm((ny, FACTORS, own), F32),
            vm((ny, FACTORS, own), F32),
            vm((ny, FACTORS, own), F32),
            vm((ny, 2 * FACTORS, own), BF16),
            pltpu.SemaphoreType.DMA((SLOTS,)),
            pltpu.SemaphoreType.DMA((2,)),
        ],
        compiler_params=pltpu.CompilerParams(collective_id=0, has_side_effects=True),
    )(motifs.T, data, loadings)


def solution(mesh):
    in_specs = (P("chan", "tm"), P("chan", "tm"), P(None, "tm"))
    out_specs = P(None, "tm")
    return jax.shard_map(
        on_device, mesh=mesh, in_specs=in_specs, out_specs=out_specs, check_vma=False
    )
```
